32 devices in a mesh: sim: 8 (over z, x), learn: 4 (over y, core).
Axes of the slice: x: 2, y: 2, z: 4, core: 2. Of those that a mesh axis runs over, the one named last changes fastest.
Arguments:
- fields: float32 [8, 64, 32, 128], P(None, 'sim', 'learn'), may hold values from -2.2 to 2.2
- diffusivity: float32 [8], replicated, may hold values from 0.5 to 1.6
- stoich: float32 [8], replicated, may hold values from -1 to 1
- basis: bfloat16 [96, 8, 64, 32, 128], P(None, None, 'sim', 'learn'), may hold values from -0.0124296114 to 0.0124296114
- gram_old: float32 [96, 96], replicated, may hold values from -6 to 6
Outputs:
- final_fields: float32 [8, 64, 32, 128], P(None, 'sim', 'learn')
- reduced: float32 [96, 8], replicated
- pod_gram: float32 [96, 96], replicated
- rhs_block: float32 [4752, 96], P('learn')
The draws below stay inside these ranges and needn't reach their ends.
All inputs are finite; a program needn't handle non-finite values.
Results may differ from the reference program's by a relative error of at most 0.0077.
Values sent between devices are 32-bit elements; how exact they have to be, the bound alone decides.
No kernel may reach another device: no remote copies, remote signals or barrier semaphores. Data moves between devices by JAX's collectives and lax.ppermute only.
A program may use at most 64 MiB of HBM per device.

```python
import math
import jax
import jax.numpy as jnp
import numpy as np
from jax import lax

NF = 8
MODES = 96
STEPS = 8
CX = 8
CY = 8
NX = 64
NY = 32
NZ = 128


def draw_fields(key, part):
    shape = (NF, NX, NY, NZ)
    along_x = jnp.arange(NX, dtype=jnp.int32)
    along_y = jnp.arange(NY, dtype=jnp.int32)
    along_z = jnp.arange(NZ, dtype=jnp.int32)
    parity = (along_x[:, None, None] + along_y[None, :, None] + along_z[None, None, :]) % 2
    alternate = 1.0 - 2.0 * parity.astype(jnp.float32)
    magnitude = jax.random.uniform(key, shape, jnp.float32, 0.6, 2.2)
    values = alternate[None] * magnitude
    return values


def draw_diffusivity(key, part):
    uniform_draw = jax.random.uniform(key, (NF,), jnp.float32, 0.0, 1.1)
    spread = jnp.max(uniform_draw) - uniform_draw
    result_values = 1.6 * jnp.exp(-spread)
    return result_values


def draw_basis(key, part):
    shape = (MODES, NF, NX, NY, NZ)
    entries = jnp.clip(jax.random.normal(key, shape, jnp.float32), -6.0, 6.0)
    along_x = jnp.arange(NX, dtype=jnp.int32) % CX
    along_y = jnp.arange(NY, dtype=jnp.int32) % CY
    edge_x = (along_x == 0) | (along_x == CX - 1)
    edge_y = (along_y == 0) | (along_y == CY - 1)
    on_face = edge_x[:, None] | edge_y[None, :]
    factor = jnp.where(on_face, 3.0, 1.0).astype(jnp.float32)
    face_count = CX * CY - max(CX - 2, 0) * max(CY - 2, 0)
    total_weight = NX // CX * (NY // CY) * (9 * face_count + CX * CY - face_count) * NF * NZ
    return (entries * factor[None, None, :, :, None] / math.sqrt(total_weight)).astype(jnp.bfloat16)


def scatter_about(stream_key, shape, scale, limit, kind=jnp.bfloat16):
    drawn = jax.random.normal(stream_key, shape, jnp.float32) * scale
    return jnp.minimum(jnp.maximum(drawn, -limit), limit).astype(kind)


def setup_inputs(seed: int = 0) -> dict:
    seeds = jax.random.split(jax.random.key(seed), 6)
    return {
        "fields": draw_fields(jax.random.fold_in(seeds[5], 71), 0),
        "diffusivity": draw_diffusivity(jax.random.fold_in(seeds[5], 71), 0),
        "stoich": jnp.clip(jax.random.uniform(seeds[2], (NF,), jnp.float32, -1.0, 1.0), -1.0, 1.0),
        "basis": draw_basis(jax.random.fold_in(seeds[5], 71), 0),
        "gram_old": scatter_about(seeds[4], (MODES, MODES), 1.0, 6.0, jnp.float32),
    }


time_step = 0.1
drift_x = 1.2
drift_y = 1.0
drift_z = 0.3
arrhenius = 2.0
activation = 1.0


def tendency(padded, diffusivity, stoich):
    centre = padded[:, 1:-1, 1:-1, 1:-1]
    east = padded[:, 2:, 1:-1, 1:-1]
    west = padded[:, :-2, 1:-1, 1:-1]
    north = padded[:, 1:-1, 2:, 1:-1]
    south = padded[:, 1:-1, :-2, 1:-1]
    upper = padded[:, 1:-1, 1:-1, 2:]
    lower = padded[:, 1:-1, 1:-1, :-2]
    laplace = east + west + north + south + upper + lower - 6.0 * centre
    advect = drift_x * 0.5 * (east - west) + drift_y * 0.5 * (north - south) + drift_z * 0.5 * (upper - lower)
    reaction = arrhenius * jnp.tanh(centre[0]) * jnp.tanh(centre[1]) * jnp.exp(-activation / (1.0 + centre[7] * centre[7]))
    return diffusivity[:, None, None, None] * laplace - advect + stoich[:, None, None, None] * reaction[None]


def pad_cells(state):
    return jnp.pad(state, ((0, 0), (1, 1), (1, 1), (1, 1)))


def pair_tables(modes):
    upper_pairs = np.triu_indices(modes)
    first_table = np.concatenate([np.zeros(modes), upper_pairs[0] + 1]).astype(np.int32)
    second_table = np.concatenate([np.arange(modes) + 1, upper_pairs[1] + 1]).astype(np.int32)
    return first_table, second_table


def reference(fields, diffusivity, stoich, basis, gram_old):
    state = fields
    snapshots = []
    for counter in range(STEPS):
        first = tendency(pad_cells(state), diffusivity, stoich)
        middle = state + time_step * first
        second = tendency(pad_cells(middle), diffusivity, stoich)
        state = state + 0.5 * time_step * (first + second)
        snapshots.append(state.astype(jnp.bfloat16).reshape(1, -1))
    stacked = jnp.concatenate(snapshots, axis=0)
    flat_basis = basis.reshape(MODES, -1)
    reduced = lax.dot_general(flat_basis, stacked, (((1,), (1,)), ((), ())), preferred_element_type=jnp.float32)
    pod_gram = gram_old + jnp.dot(reduced, reduced.T, precision=lax.Precision.HIGHEST, preferred_element_type=jnp.float32)
    widened = jnp.concatenate([jnp.ones((1, STEPS), jnp.float32), reduced], axis=0)
    first_table, second_table = pair_tables(MODES)
    features = widened[first_table, :-1] * widened[second_table, :-1]
    changes = reduced[:, 1:] - reduced[:, :-1]
    rhs_block = jnp.dot(features, changes.T, precision=lax.Precision.HIGHEST, preferred_element_type=jnp.float32)
    return state, reduced, pod_gram, rhs_block
```

```python
import functools

import jax
import jax.numpy as jnp
import numpy as np
from jax import lax
from jax.experimental import pallas as pl
from jax.experimental.pallas import tpu as pltpu
from jax.sharding import PartitionSpec as P

STEPS = 8

time_step = 0.1
drift_x = 1.2
drift_y = 1.0
drift_z = 0.3
arrhenius = 2.0
activation = 1.0

BOTH = ("sim", "learn")
VMEM = pl.BlockSpec(memory_space=pltpu.VMEM)
WIDE = 56 * 1024 * 1024


def both_ways(pairs):
    return [(a, b) for a, b in pairs] + [(b, a) for a, b in pairs]


def swaps(ns, nl):
    x_even = both_ways([(s * nl + l, (s + 1) * nl + l) for s in range(0, ns, 2) for l in range(nl)])
    x_odd = [(s * nl + l, (s + 1) * nl + l) for s in range(1, ns - 1, 2) for l in range(nl)]
    x_odd += [(s * nl + l, s * nl + l + 1) for s in (0, ns - 1) for l in range(0, nl, 2)]
    y_even = both_ways([(s * nl + l, s * nl + l + 1) for s in range(ns) for l in range(0, nl, 2)])
    y_odd = [(s * nl + l, s * nl + l + 1) for s in range(ns) for l in range(1, nl - 1, 2)]
    y_odd += [(s * nl, s * nl + nl - 1) for s in range(ns)]
    return x_even, both_ways(x_odd), y_even, both_ways(y_odd)


def corner_cells(reach):
    return [(d, e) for d in range(1, reach + 1) for e in range(1, reach + 1 - d)]


def pack_kernel(cx, cy, xa_ref, xb_ref, to_a_ref, to_b_ref):
    nf = to_a_ref.shape[1]
    even_s = lax.rem(lax.axis_index("sim"), 2) == 0
    even_l = lax.rem(lax.axis_index("learn"), 2) == 0
    cells = corner_cells(min(cx, cy))
    for side, brick in enumerate((xa_ref, xb_ref)):
        is_east = even_s if side == 0 else jnp.logical_not(even_s)
        for n, (d, e) in enumerate(cells):
            row = jnp.where(is_east, d - 1, cx - d) * cy
            high, low = row + cy - e, row + e - 1
            for out_ref, north in ((to_a_ref, even_l), (to_b_ref, jnp.logical_not(even_l))):
                start = jnp.where(north, high, low)
                out_ref[side * len(cells) + n] = brick[pl.ds(start, nf, stride=cx * cy), :]


def pack_corners(xa, xb, cx, cy, nf, nz):
    count = 2 * len(corner_cells(min(cx, cy)))
    shape = jax.ShapeDtypeStruct((count, nf, nz), jnp.float32)
    return pl.pallas_call(
        functools.partial(pack_kernel, cx, cy),
        out_shape=(shape, shape),
        in_specs=[VMEM, VMEM],
        out_specs=(VMEM, VMEM),
        name="pack_corners",
    )(xa, xb)


def rows_loop(start, count, group, body):
    main = count // group

    def trip(i, carry):
        for k in range(group):
            body(start + i * group + k)
        return carry

    lax.fori_loop(0, main, trip, 0)
    for k in range(main * group, count):
        body(start + k)


def round_kernel(
    cx, cy, steps, own_ref, xa_ref, xb_ref, ya_ref, yb_ref, ca_ref, cb_ref, dif_ref, sto_ref,
    state_ref, snap_ref, u_ref, m_ref, rate_ref,
):
    nf, nz = dif_ref.shape
    reach = 2 * steps
    wide_x, wide_y = cx + 2 * reach, cy + 2 * reach
    s, l = lax.axis_index("sim"), lax.axis_index("learn")
    ns, nl = lax.axis_size("sim"), lax.axis_size("learn")
    even_s, even_l = lax.rem(s, 2) == 0, lax.rem(l, 2) == 0
    has_west, has_east = s > 0, s < ns - 1
    has_south, has_north = l > 0, l < nl - 1

    def column(x, y):
        return pl.multiple_of((x * wide_y + y) * nf, nf)

    zero = jnp.zeros((nf, nz), jnp.float32)

    def clear(i, carry):
        for k in range(wide_y):
            u_ref[pl.ds(column(i, k), nf), :] = zero
            m_ref[pl.ds(column(i, k), nf), :] = zero
        return carry

    lax.fori_loop(0, wide_x, clear, 0)

    def place(ref, x0, y0, first_x, first_y, size_x, size_y):
        def trip(i, carry):
            for j in range(size_y):
                value = ref[pl.ds((first_x + i) * cy + first_y + j, nf, stride=cx * cy), :]
                u_ref[pl.ds(column(x0 + i, y0 + j), nf), :] = value
            return carry

        lax.fori_loop(0, size_x, trip, 0)

    place(own_ref, reach, reach, 0, 0, cx, cy)
    for ref, is_east in ((xa_ref, even_s), (xb_ref, jnp.logical_not(even_s))):

        @pl.when(jnp.where(is_east, has_east, has_west))
        def _(ref=ref, is_east=is_east):
            place(ref, jnp.where(is_east, reach + cx, 0), reach, jnp.where(is_east, 0, cx - reach), 0, reach, cy)

    for ref, is_north in ((ya_ref, even_l), (yb_ref, jnp.logical_not(even_l))):

        @pl.when(jnp.where(is_north, has_north, has_south))
        def _(ref=ref, is_north=is_north):
            place(ref, reach, jnp.where(is_north, reach + cy, 0), 0, jnp.where(is_north, 0, cy - reach), cx, reach)

    cells = corner_cells(reach)
    for ref, is_north in ((ca_ref, even_l), (cb_ref, jnp.logical_not(even_l))):
        for side, is_east in ((0, even_s), (1, jnp.logical_not(even_s))):
            has_y = jnp.where(is_north, has_north, has_south)
            has_x = jnp.where(is_east, has_east, has_west)

            @pl.when(jnp.logical_and(has_x, has_y))
            def _(ref=ref, is_north=is_north, side=side, is_east=is_east):
                for n, (d, e) in enumerate(cells):
                    x = jnp.where(is_east, reach + cx + d - 1, reach - d)
                    y = jnp.where(is_north, reach + cy + e - 1, reach - e)
                    u_ref[pl.ds(column(x, y), nf), :] = ref[side * len(cells) + n]

    diffusivity, stoich = dif_ref[...], sto_ref[...]
    lane = lax.broadcasted_iota(jnp.int32, (nf, nz), 1)

    def coefficients(dt):
        return (
            1.0 * (dt / time_step) - 6.0 * dt * diffusivity,
            dt * (diffusivity - 0.5 * drift_x),
            dt * (diffusivity + 0.5 * drift_x),
            dt * (diffusivity - 0.5 * drift_y),
            dt * (diffusivity + 0.5 * drift_y),
            jnp.where(lane < nz - 1, dt * (diffusivity - 0.5 * drift_z), 0.0),
            jnp.where(lane > 0, dt * (diffusivity + 0.5 * drift_z), 0.0),
            dt * arrhenius * stoich,
        )

    in_south = jnp.where(has_south, 1.0, 0.0)
    in_north = jnp.where(has_north, 1.0, 0.0)

    def stage(src, dst, old, r, coefs):
        cc, ce, cw, cn, cs, cu, cl, ck = coefs
        y_first, width = reach - r, cy + 2 * r
        packs = -(-width // nf)

        def rate_row(x):
            for p in range(packs):
                base = (x * wide_y + y_first + p * nf) * nf
                u0 = src[pl.ds(base, nf, stride=nf), :]
                u1 = src[pl.ds(base + 1, nf, stride=nf), :]
                u7 = src[pl.ds(base + 7, nf, stride=nf), :]
                rate = jnp.tanh(u0) * jnp.tanh(u1) * jnp.exp(-activation / (1.0 + u7 * u7))
                rate_ref[pl.ds(pl.multiple_of(x * (wide_y + nf) + p * nf, nf), nf), :] = rate

        rows_loop(reach - r, cx + 2 * r, max(1, 12 // packs), rate_row)

        def columns_row(x):
            here = [src[pl.ds(column(x, y_first - 1 + j), nf), :] for j in range(2)]
            for j in range(width):
                y = y_first + j
                south, centre = here
                north = src[pl.ds(column(x, y + 1), nf), :]
                value = cc * centre + cn * north + cs * south
                value += ce * src[pl.ds(column(x + 1, y), nf), :] + cw * src[pl.ds(column(x - 1, y), nf), :]
                value += cu * pltpu.roll(centre, nz - 1, 1) + cl * pltpu.roll(centre, 1, 1)
                value += ck * rate_ref[pl.ds(x * (wide_y + nf) + j, nf, stride=0), :]
                if old is not None:
                    value += 0.5 * old[pl.ds(column(x, y), nf), :]
                if y < reach:
                    value *= in_south
                if y >= reach + cy:
                    value *= in_north
                dst[pl.ds(column(x, y), nf), :] = value
                here = [centre, north]

        low = jnp.where(has_west, reach - r, reach)
        high = jnp.where(has_east, reach + cx + r, reach + cx)

        def trip(x, carry):
            columns_row(x)
            return carry

        lax.fori_loop(low, high, trip, 0)

    whole, half = coefficients(time_step), coefficients(0.5 * time_step)
    for t in range(steps):
        r = reach - 1 - 2 * t
        stage(u_ref, m_ref, None, r, whole)
        stage(m_ref, u_ref, u_ref, r - 1, half)
        for x in range(cx):
            for f in range(nf):
                value = u_ref[pl.ds(((reach + x) * wide_y + reach) * nf + f, cy, stride=nf), :]
                snap_ref[f * cx + x, pl.ds(t * cy, cy), :] = value
                if t == steps - 1:
                    state_ref[pl.ds((f * cx + x) * cy, cy), :] = value


def advance(state, neighbours, corners, dif, sto, steps):
    nf, cx, cy, nz = state.shape
    wide = (cx + 4 * steps) * (cy + 4 * steps)
    flat = [a.reshape(nf * cx * cy, nz) for a in (state, *neighbours)]
    new, snaps = pl.pallas_call(
        functools.partial(round_kernel, cx, cy, steps),
        out_shape=(
            jax.ShapeDtypeStruct((nf * cx * cy, nz), jnp.float32),
            jax.ShapeDtypeStruct((nf * cx, steps * cy, nz), jnp.float32),
        ),
        in_specs=[VMEM] * 9,
        out_specs=(VMEM, VMEM),
        scratch_shapes=[
            pltpu.VMEM((wide * nf + 8 * nf, nz), jnp.float32),
            pltpu.VMEM((wide * nf + 8 * nf, nz), jnp.float32),
            pltpu.VMEM(((cx + 4 * steps) * (cy + 4 * steps + nf), nz), jnp.float32),
        ],
        name="advance",
    )(*flat, *corners, dif, sto)
    return new.reshape(state.shape), snaps


def project_kernel(cy, steps, basis_ref, snap_ref, out_ref, acc_ref):
    modes, pair, cells, nz = basis_ref.shape
    cx = cells // cy
    step = pl.program_id(0)

    @pl.when(step == 0)
    def _():
        acc_ref[...] = jnp.zeros_like(acc_ref)

    total = None
    for p in range(cx // 2):
        left = [basis_ref[:, f, pl.ds(p * 2 * cy, 2 * cy), :].reshape(modes * 2 * cy, nz) for f in range(pair)]
        right = [
            snap_ref[pl.ds(f * cx + 2 * p, 2)].reshape(2 * steps * cy, nz).astype(jnp.bfloat16) for f in range(pair)
        ]
        term = lax.dot_general(
            jnp.concatenate(left, axis=1),
            jnp.concatenate(right, axis=1),
            (((1,), (1,)), ((), ())),
            preferred_element_type=jnp.float32,
        )
        total = term if total is None else total + term
    acc_ref[...] += total

    @pl.when(step == pl.num_programs(0) - 1)
    def _():
        columns = 2 * steps * cy
        row = lax.broadcasted_iota(jnp.int32, (2 * cy, columns), 0)
        column = lax.broadcasted_iota(jnp.int32, (2 * cy, columns), 1)
        same = (row // cy == column // (steps * cy)) & (row % cy == column % cy)
        kept = acc_ref[...].reshape(modes, 2 * cy, columns) * same.astype(jnp.float32)[None]
        kept = jnp.sum(kept, axis=1)
        which = lax.broadcasted_iota(jnp.int32, (steps, columns), 0)
        column = lax.broadcasted_iota(jnp.int32, (steps, columns), 1)
        gather = (column // cy % steps == which).astype(jnp.float32)
        out_ref[...] = lax.dot_general(
            gather, kept, (((1,), (1,)), ((), ())),
            precision=lax.Precision.HIGHEST, preferred_element_type=jnp.float32,
        )


def project(basis, snaps, steps):
    modes, nf, cx, cy, nz = basis.shape
    pair = 2
    return pl.pallas_call(
        functools.partial(project_kernel, cy, steps),
        out_shape=jax.ShapeDtypeStruct((steps, modes), jnp.float32),
        grid=(nf // pair,),
        in_specs=[
            pl.BlockSpec((modes, pair, cx * cy, nz), lambda i: (0, i, 0, 0)),
            pl.BlockSpec((pair * cx, steps * cy, nz), lambda i: (i, 0, 0)),
        ],
        out_specs=pl.BlockSpec((steps, modes), lambda i: (0, 0)),
        scratch_shapes=[pltpu.VMEM((modes * 2 * cy, 2 * steps * cy), jnp.float32)],
        compiler_params=pltpu.CompilerParams(vmem_limit_bytes=WIDE),
        name="project",
    )(basis.reshape(modes, nf, cx * cy, nz), snaps)


def pair_tables(modes):
    upper_pairs = np.triu_indices(modes)
    first_table = np.concatenate([np.zeros(modes), upper_pairs[0] + 1]).astype(np.int32)
    second_table = np.concatenate([np.arange(modes) + 1, upper_pairs[1] + 1]).astype(np.int32)
    return (first_table, second_table)


def body(fields, diffusivity, stoich, basis, gram_old):
    modes = basis.shape[0]
    nf, cx, cy, nz = fields.shape
    ns, nl = lax.axis_size("sim"), lax.axis_size("learn")
    steps = min(cx, cy) // 2
    x_even, x_odd, y_even, y_odd = swaps(ns, nl)
    dif = jnp.broadcast_to(diffusivity[:, None], (nf, nz))
    sto = jnp.broadcast_to(stoich[:, None], (nf, nz))
    state = fields
    parts = []
    for _ in range(STEPS // steps):
        ya = lax.ppermute(state, BOTH, y_even)
        yb = lax.ppermute(state, BOTH, y_odd)
        xa = lax.ppermute(state, BOTH, x_even)
        xb = lax.ppermute(state, BOTH, x_odd)
        to_a, to_b = pack_corners(xa.reshape(-1, nz), xb.reshape(-1, nz), cx, cy, nf, nz)
        ca = lax.ppermute(to_a, BOTH, y_even)
        cb = lax.ppermute(to_b, BOTH, y_odd)
        state, snaps = advance(state, (xa, xb, ya, yb), (ca, cb), dif, sto, steps)
        parts.append(project(basis, snaps, steps))
    local = jnp.concatenate(parts, axis=0)
    sent = jnp.broadcast_to(local[None], (ns * nl, *local.shape))
    reduced_t = jnp.sum(lax.all_to_all(sent, BOTH, 0, 0), axis=0)
    reduced = reduced_t.T
    pod_gram = gram_old + lax.dot_general(
        reduced_t, reduced_t, (((0,), (0,)), ((), ())),
        precision=lax.Precision.HIGHEST, preferred_element_type=jnp.float32,
    )
    widened = jnp.concatenate([jnp.ones((1, STEPS), jnp.float32), reduced], axis=0)
    first_table, second_table = pair_tables(modes)
    block_rows = first_table.shape[0] // nl
    start = lax.axis_index("learn") * block_rows
    first_rows = lax.dynamic_slice_in_dim(jnp.asarray(first_table), start, block_rows)
    second_rows = lax.dynamic_slice_in_dim(jnp.asarray(second_table), start, block_rows)
    columns = jnp.arange(modes + 1, dtype=jnp.int32)
    pick_first = (first_rows[:, None] == columns[None, :]).astype(jnp.float32)
    pick_second = (second_rows[:, None] == columns[None, :]).astype(jnp.float32)
    earlier = widened[:, :-1]
    left_part = jnp.dot(
        pick_first, earlier, precision=lax.Precision.HIGHEST, preferred_element_type=jnp.float32
    )
    right_part = jnp.dot(
        pick_second, earlier, precision=lax.Precision.HIGHEST, preferred_element_type=jnp.float32
    )
    features = left_part * right_part
    changes = reduced[:, 1:] - reduced[:, :-1]
    rhs_block = jnp.dot(
        features, changes.T, precision=lax.Precision.HIGHEST, preferred_element_type=jnp.float32
    )
    return (state, reduced, pod_gram, rhs_block)


def solution(mesh):
    in_specs = (P(None, "sim", "learn", None), P(), P(), P(None, None, "sim", "learn", None), P())
    out_specs = (P(None, "sim", "learn", None), P(), P(), P("learn", None))
    return jax.shard_map(body, mesh=mesh, in_specs=in_specs, out_specs=out_specs, check_vma=False)
```

```python
import functools

import jax
import jax.numpy as jnp
import numpy as np
from jax import lax
from jax.experimental import pallas as pl
from jax.experimental.pallas import tpu as pltpu
from jax.sharding import PartitionSpec as P

STEPS = 8

time_step = 0.1
drift_x = 1.2
drift_y = 1.0
drift_z = 0.3
arrhenius = 2.0
activation = 1.0

BOTH = ("sim", "learn")
VMEM = pl.BlockSpec(memory_space=pltpu.VMEM)
WIDE = 56 * 1024 * 1024


def both_ways(pairs):
    return [(a, b) for a, b in pairs] + [(b, a) for a, b in pairs]


def swaps(ns, nl):
    x_even = both_ways([(s * nl + l, (s + 1) * nl + l) for s in range(0, ns, 2) for l in range(nl)])
    x_odd = [(s * nl + l, (s + 1) * nl + l) for s in range(1, ns - 1, 2) for l in range(nl)]
    x_odd += [(s * nl + l, s * nl + l + 1) for s in (0, ns - 1) for l in range(0, nl, 2)]
    y_even = both_ways([(s * nl + l, s * nl + l + 1) for s in range(ns) for l in range(0, nl, 2)])
    y_odd = [(s * nl + l, s * nl + l + 1) for s in range(ns) for l in range(1, nl - 1, 2)]
    y_far = y_odd + [(s * nl + l, (s + 1) * nl + l) for s in range(0, ns, 2) for l in (0, nl - 1)]
    y_odd = y_odd + [(s * nl, s * nl + nl - 1) for s in range(ns)]
    return x_even, both_ways(x_odd), y_even, both_ways(y_odd), both_ways(y_far)


def in_vmem(*arrays):
    return [pltpu.with_memory_space_constraint(a, pltpu.VMEM) for a in arrays]


def corner_runs(reach):
    runs, first = [], 0
    for d in range(1, reach):
        runs.append((d, reach - d, first))
        first += reach - d
    return runs, first


def each_case(first, second, body):
    for a in (True, False):
        for b in (True, False):

            @pl.when(jnp.logical_and(first == a, second == b))
            def _(a=a, b=b):
                body(a, b)


def columns_kernel(cx, cy, native_ref, out_ref):
    nf = native_ref.shape[0] // (cx * cy)
    for c in range(cx * cy):
        out_ref[pl.ds(c * nf, nf), :] = native_ref[pl.ds(c, nf, stride=cx * cy), :]


def to_columns(fields):
    nf, cx, cy, nz = fields.shape
    return pl.pallas_call(
        functools.partial(columns_kernel, cx, cy),
        out_shape=pltpu.VMEM((cx * cy * nf, nz), jnp.float32),
        in_specs=[VMEM],
        out_specs=VMEM,
        name="to_columns",
    )(fields.reshape(nf * cx * cy, nz))


def pack_kernel(cx, cy, nf, xa_ref, xb_ref, to_a_ref, to_b_ref):
    runs, size = corner_runs(min(cx, cy))
    even_s = lax.rem(lax.axis_index("sim"), 2) == 0
    even_l = lax.rem(lax.axis_index("learn"), 2) == 0

    def copy(s_is_even, l_is_even):
        for side, brick in enumerate((xa_ref, xb_ref)):
            is_east = s_is_even == (side == 0)
            for out_ref, north in ((to_a_ref, l_is_even), (to_b_ref, not l_is_even)):
                for d, count, first in runs:
                    x = d - 1 if is_east else cx - d
                    y = cy - count if north else 0
                    rows = brick[pl.ds((x * cy + y) * nf, count * nf), :]
                    out_ref[pl.ds((side * size + first) * nf, count * nf), :] = rows

    each_case(even_s, even_l, copy)


def pack_corners(xa, xb, cx, cy, nf):
    nz = xa.shape[1]
    size = 2 * corner_runs(min(cx, cy))[1]
    shape = pltpu.VMEM((size * nf, nz), jnp.float32)
    return pl.pallas_call(
        functools.partial(pack_kernel, cx, cy, nf),
        out_shape=(shape, shape),
        in_specs=[VMEM, VMEM],
        out_specs=(VMEM, VMEM),
        name="pack_corners",
    )(*in_vmem(xa, xb))


def round_kernel(
    cx, cy, nf, steps, last, own_ref, xa_ref, xb_ref, ya_ref, yb_ref, ca_ref, cb_ref, dif_ref, sto_ref,
    state_ref, snap_ref, u_ref, m_ref, rate_ref,
):
    nz = own_ref.shape[1]
    reach = 2 * steps
    wide_x, wide_y = cx + 2 * reach, cy + 2 * reach
    s, l = lax.axis_index("sim"), lax.axis_index("learn")
    ns, nl = lax.axis_size("sim"), lax.axis_size("learn")
    even_s, even_l = lax.rem(s, 2) == 0, lax.rem(l, 2) == 0
    has_west, has_east = s > 0, s < ns - 1
    has_south, has_north = l > 0, l < nl - 1

    def place(ref, x0, y0):
        for i in range(cx):
            u_ref[pl.ds(((x0 + i) * wide_y + y0) * nf, cy * nf), :] = ref[pl.ds(i * cy * nf, cy * nf), :]

    def clear(x0, x1, y0, y1):
        zeros = jnp.zeros(((y1 - y0) * nf, nz), jnp.float32)

        def trip(x, carry):
            for ref in (u_ref, m_ref):
                ref[pl.ds(pl.multiple_of((x * wide_y + y0) * nf, nf), (y1 - y0) * nf), :] = zeros
            return carry

        lax.fori_loop(x0, x1, trip, 0)

    place(own_ref, reach, reach)
    runs, size = corner_runs(reach)

    def receive(s_is_even, l_is_even):
        for side, brick in enumerate((xa_ref, xb_ref)):
            is_east = s_is_even == (side == 0)

            @pl.when(has_east if is_east else has_west)
            def _(brick=brick, is_east=is_east):
                place(brick, reach + cx if is_east else 0, reach)

        for corner, brick, north in ((ca_ref, ya_ref, l_is_even), (cb_ref, yb_ref, not l_is_even)):

            @pl.when(has_north if north else has_south)
            def _(corner=corner, brick=brick, north=north):
                place(brick, reach, reach + cy if north else 0)
                for side in range(2):
                    is_east = s_is_even == (side == 0)
                    for d, count, first in runs:
                        x = reach + cx + d - 1 if is_east else reach - d
                        y = reach + cy if north else reach - count
                        rows = corner[pl.ds((side * size + first) * nf, count * nf), :]
                        u_ref[pl.ds((x * wide_y + y) * nf, count * nf), :] = rows

    each_case(even_s, even_l, receive)
    pl.when(jnp.logical_not(has_west))(lambda: clear(0, reach, 0, wide_y))
    pl.when(jnp.logical_not(has_east))(lambda: clear(reach + cx, wide_x, 0, wide_y))
    pl.when(jnp.logical_not(has_south))(lambda: clear(0, wide_x, 0, reach))
    pl.when(jnp.logical_not(has_north))(lambda: clear(0, wide_x, reach + cy, wide_y))

    field = lax.broadcasted_iota(jnp.int32, (nf, nz), 0)
    lane = lax.broadcasted_iota(jnp.int32, (nf, nz), 1)
    diffusivity, stoich = jnp.zeros((nf, nz), jnp.float32), jnp.zeros((nf, nz), jnp.float32)
    for f in range(nf):
        diffusivity = jnp.where(field == f, dif_ref[f], diffusivity)
        stoich = jnp.where(field == f, sto_ref[f], stoich)

    def coefficients(dt):
        return (
            1.0 * (dt / time_step) - 6.0 * dt * diffusivity,
            dt * (diffusivity - 0.5 * drift_x),
            dt * (diffusivity + 0.5 * drift_x),
            dt * (diffusivity - 0.5 * drift_y),
            dt * (diffusivity + 0.5 * drift_y),
            jnp.where(lane < nz - 1, dt * (diffusivity - 0.5 * drift_z), 0.0),
            jnp.where(lane > 0, dt * (diffusivity + 0.5 * drift_z), 0.0),
            dt * arrhenius * stoich,
        )

    in_south = jnp.where(has_south, 1.0, 0.0)
    in_north = jnp.where(has_north, 1.0, 0.0)

    def rows_block(src, dst, old, coefs, rows):
        cc, ce, cw, cn, cs, cu, cl, ck = coefs

        def load(x, y):
            return src[pl.ds((x * wide_y + y) * nf, nf), :]

        for k, (x, beyond) in enumerate(rows):
            y_first, width = reach - beyond, cy + 2 * beyond
            for p in range(0, width, nf):
                base = (x * wide_y + y_first + p) * nf
                u0 = src[pl.ds(base, nf, stride=nf), :]
                u1 = src[pl.ds(base + 1, nf, stride=nf), :]
                u7 = src[pl.ds(base + 7, nf, stride=nf), :]
                rate = jnp.tanh(u0) * jnp.tanh(u1) * jnp.exp(-activation / (1.0 + u7 * u7))
                rate_ref[pl.ds(k * (wide_y + nf) + p, nf), :] = rate
        for k, (x, beyond) in enumerate(rows):
            y_first, width = reach - beyond, cy + 2 * beyond
            south, centre = load(x, y_first - 1), load(x, y_first)
            for j in range(width):
                y = y_first + j
                north = load(x, y + 1)
                value = cc * centre + cn * north + cs * south
                value += ce * load(x + 1, y) + cw * load(x - 1, y)
                value += cu * pltpu.roll(centre, nz - 1, 1) + cl * pltpu.roll(centre, 1, 1)
                value += ck * rate_ref[pl.ds(k * (wide_y + nf) + j, nf, stride=0), :]
                if old is not None:
                    value += 0.5 * old[pl.ds((x * wide_y + y) * nf, nf), :]
                if y < reach:
                    value *= in_south
                if y >= reach + cy:
                    value *= in_north
                dst[pl.ds((x * wide_y + y) * nf, nf), :] = value
                south, centre = centre, north

    def stage(src, dst, old, r, coefs):
        group = 4

        def trip(i, carry):
            x0 = reach + i * group
            rows_block(src, dst, old, coefs, [(x0 + k, r) for k in range(group)])
            return carry

        lax.fori_loop(0, cx // group, trip, 0)
        if r:

            @pl.when(has_west)
            def _():
                rows_block(src, dst, old, coefs, [(reach - d, r - d) for d in range(1, r + 1)])

            @pl.when(has_east)
            def _():
                rows_block(src, dst, old, coefs, [(reach + cx - 1 + d, r - d) for d in range(1, r + 1)])

    whole, half = coefficients(time_step), coefficients(0.5 * time_step)
    for t in range(steps):
        r = reach - 1 - 2 * t
        stage(u_ref, m_ref, None, r, whole)
        stage(m_ref, u_ref, u_ref, r - 1, half)
        for x in range(cx):
            for f in range(nf):
                value = u_ref[pl.ds(((reach + x) * wide_y + reach) * nf + f, cy, stride=nf), :]
                snap_ref[f * cx + x, pl.ds(t * cy, cy), :] = value
                if last and t == steps - 1:
                    state_ref[pl.ds((f * cx + x) * cy, cy), :] = value
    if not last:
        for i in range(cx):
            rows = u_ref[pl.ds(((reach + i) * wide_y + reach) * nf, cy * nf), :]
            state_ref[pl.ds(i * cy * nf, cy * nf), :] = rows


def advance(bricks, corners, dif, sto, cx, cy, nf, steps, last):
    nz = bricks[0].shape[1]
    wide = (cx + 4 * steps) * (cy + 4 * steps)
    rows = max(cx, 2 * steps) * (cy + 4 * steps + nf)
    shape = (nf * cx * cy, nz)
    scalars = pl.BlockSpec(memory_space=pltpu.SMEM)
    return pl.pallas_call(
        functools.partial(round_kernel, cx, cy, nf, steps, last),
        out_shape=(
            jax.ShapeDtypeStruct(shape, jnp.float32) if last else pltpu.VMEM(shape, jnp.float32),
            pltpu.VMEM((nf * cx, steps * cy, nz), jnp.float32),
        ),
        in_specs=[VMEM] * 7 + [scalars] * 2,
        out_specs=(VMEM, VMEM),
        scratch_shapes=[
            pltpu.VMEM((wide * nf, nz), jnp.float32),
            pltpu.VMEM((wide * nf, nz), jnp.float32),
            pltpu.VMEM((rows, nz), jnp.float32),
        ],
        name="advance",
    )(*in_vmem(*bricks, *corners), dif, sto)


def project_kernel(cy, steps, basis_ref, snap_ref, out_ref, acc_ref):
    modes, pair, cells, nz = basis_ref.shape
    cx = cells // cy
    step = pl.program_id(0)

    @pl.when(step == 0)
    def _():
        acc_ref[...] = jnp.zeros_like(acc_ref)

    total = None
    for p in range(cx // 2):
        left = [basis_ref[:, f, pl.ds(p * 2 * cy, 2 * cy), :].reshape(modes * 2 * cy, nz) for f in range(pair)]
        right = [
            snap_ref[pl.ds(f * cx + 2 * p, 2)].reshape(2 * steps * cy, nz).astype(jnp.bfloat16) for f in range(pair)
        ]
        term = lax.dot_general(
            jnp.concatenate(left, axis=1),
            jnp.concatenate(right, axis=1),
            (((1,), (1,)), ((), ())),
            preferred_element_type=jnp.float32,
        )
        total = term if total is None else total + term
    acc_ref[...] += total

    @pl.when(step == pl.num_programs(0) - 1)
    def _():
        columns = 2 * steps * cy
        row = lax.broadcasted_iota(jnp.int32, (2 * cy, columns), 0)
        column = lax.broadcasted_iota(jnp.int32, (2 * cy, columns), 1)
        same = (row // cy == column // (steps * cy)) & (row % cy == column % cy)
        kept = acc_ref[...].reshape(modes, 2 * cy, columns) * same.astype(jnp.float32)[None]
        kept = jnp.sum(kept, axis=1)
        which = lax.broadcasted_iota(jnp.int32, (steps, columns), 0)
        column = lax.broadcasted_iota(jnp.int32, (steps, columns), 1)
        gather = (column // cy % steps == which).astype(jnp.float32)
        out_ref[...] = lax.dot_general(
            gather, kept, (((1,), (1,)), ((), ())),
            precision=lax.Precision.HIGHEST, preferred_element_type=jnp.float32,
        )


def project(basis, snaps, steps):
    modes, nf, cx, cy, nz = basis.shape
    pair = 2
    return pl.pallas_call(
        functools.partial(project_kernel, cy, steps),
        out_shape=jax.ShapeDtypeStruct((steps, modes), jnp.float32),
        grid=(nf // pair,),
        in_specs=[
            pl.BlockSpec((modes, pair, cx * cy, nz), lambda i: (0, i, 0, 0)),
            pl.BlockSpec((pair * cx, steps * cy, nz), lambda i: (i, 0, 0)),
        ],
        out_specs=pl.BlockSpec((steps, modes), lambda i: (0, 0)),
        scratch_shapes=[pltpu.VMEM((modes * 2 * cy, 2 * steps * cy), jnp.float32)],
        compiler_params=pltpu.CompilerParams(vmem_limit_bytes=WIDE),
        name="project",
    )(basis.reshape(modes, nf, cx * cy, nz), *in_vmem(snaps))


def pair_tables(modes):
    upper_pairs = np.triu_indices(modes)
    first_table = np.concatenate([np.zeros(modes), upper_pairs[0] + 1]).astype(np.int32)
    second_table = np.concatenate([np.arange(modes) + 1, upper_pairs[1] + 1]).astype(np.int32)
    return (first_table, second_table)


def body(fields, diffusivity, stoich, basis, gram_old):
    modes = basis.shape[0]
    nf, cx, cy, nz = fields.shape
    ns, nl = lax.axis_size("sim"), lax.axis_size("learn")
    steps = min(cx, cy) // 2
    x_even, x_odd, y_even, y_odd, y_far = swaps(ns, nl)
    state = to_columns(fields)
    rounds = STEPS // steps
    parts = []
    for n in range(rounds):
        ya = lax.ppermute(state, BOTH, y_even)
        yb = lax.ppermute(state, BOTH, y_odd)
        xa = lax.ppermute(state, BOTH, x_even)
        xb = lax.ppermute(state, BOTH, x_odd)
        to_a, to_b = pack_corners(xa, xb, cx, cy, nf)
        ca = lax.ppermute(to_a, BOTH, y_even)
        cb = lax.ppermute(to_b, BOTH, y_far)
        bricks = (state, xa, xb, ya, yb)
        state, snaps = advance(bricks, (ca, cb), diffusivity, stoich, cx, cy, nf, steps, n == rounds - 1)
        parts.append(project(basis, snaps, steps))
    state = state.reshape(fields.shape)
    local = jnp.concatenate(parts, axis=0)
    sent = jnp.broadcast_to(local[None], (ns * nl, *local.shape))
    reduced_t = jnp.sum(lax.all_to_all(sent, BOTH, 0, 0), axis=0)
    reduced = reduced_t.T
    pod_gram = gram_old + lax.dot_general(
        reduced_t, reduced_t, (((0,), (0,)), ((), ())),
        precision=lax.Precision.HIGHEST, preferred_element_type=jnp.float32,
    )
    widened = jnp.concatenate([jnp.ones((1, STEPS), jnp.float32), reduced], axis=0)
    first_table, second_table = pair_tables(modes)
    block_rows = first_table.shape[0] // nl
    start = lax.axis_index("learn") * block_rows
    first_rows = lax.dynamic_slice_in_dim(jnp.asarray(first_table), start, block_rows)
    second_rows = lax.dynamic_slice_in_dim(jnp.asarray(second_table), start, block_rows)
    columns = jnp.arange(modes + 1, dtype=jnp.int32)
    pick_first = (first_rows[:, None] == columns[None, :]).astype(jnp.float32)
    pick_second = (second_rows[:, None] == columns[None, :]).astype(jnp.float32)
    earlier = widened[:, :-1]
    left_part = jnp.dot(
        pick_first, earlier, precision=lax.Precision.HIGHEST, preferred_element_type=jnp.float32
    )
    right_part = jnp.dot(
        pick_second, earlier, precision=lax.Precision.HIGHEST, preferred_element_type=jnp.float32
    )
    features = left_part * right_part
    changes = reduced[:, 1:] - reduced[:, :-1]
    rhs_block = jnp.dot(
        features, changes.T, precision=lax.Precision.HIGHEST, preferred_element_type=jnp.float32
    )
    return (state, reduced, pod_gram, rhs_block)


def solution(mesh):
    in_specs = (P(None, "sim", "learn", None), P(), P(), P(None, None, "sim", "learn", None), P())
    out_specs = (P(None, "sim", "learn", None), P(), P(), P("learn", None))
    return jax.shard_map(body, mesh=mesh, in_specs=in_specs, out_specs=out_specs, check_vma=False)
```

```python
import functools

import jax
import jax.numpy as jnp
import numpy as np
from jax import lax
from jax.experimental import pallas as pl
from jax.experimental.pallas import tpu as pltpu
from jax.sharding import PartitionSpec as P

STEPS = 8

time_step = 0.1
drift_x = 1.2
drift_y = 1.0
drift_z = 0.3
arrhenius = 2.0
activation = 1.0

BOTH = ("sim", "learn")
VMEM = pl.BlockSpec(memory_space=pltpu.VMEM)
MIB = 1024 * 1024


def both_ways(pairs):
    return [(a, b) for a, b in pairs] + [(b, a) for a, b in pairs]


def swaps(ns, nl):
    x_even = both_ways([(s * nl + l, (s + 1) * nl + l) for s in range(0, ns, 2) for l in range(nl)])
    x_odd = [(s * nl + l, (s + 1) * nl + l) for s in range(1, ns - 1, 2) for l in range(nl)]
    x_odd += [(s * nl + l, s * nl + l + 1) for s in (0, ns - 1) for l in range(0, nl, 2)]
    y_even = both_ways([(s * nl + l, s * nl + l + 1) for s in range(ns) for l in range(0, nl, 2)])
    y_odd = [(s * nl + l, s * nl + l + 1) for s in range(ns) for l in range(1, nl - 1, 2)]
    y_far = y_odd + [(s * nl + l, (s + 1) * nl + l) for s in range(0, ns, 2) for l in (0, nl - 1)]
    y_odd = y_odd + [(s * nl, s * nl + nl - 1) for s in range(ns)]
    return x_even, both_ways(x_odd), y_even, both_ways(y_odd), both_ways(y_far)


def in_vmem(*arrays):
    return [pltpu.with_memory_space_constraint(a, pltpu.VMEM) for a in arrays]


def corner_runs(reach):
    runs, first = [], 0
    for d in range(1, reach):
        runs.append((d, reach - d, first))
        first += reach - d
    return runs, first


def each_case(first, second, body):
    for a in (True, False):
        for b in (True, False):

            @pl.when(jnp.logical_and(first == a, second == b))
            def _(a=a, b=b):
                body(a, b)


def columns_kernel(cx, cy, native_ref, out_ref):
    nf = native_ref.shape[0] // (cx * cy)
    for c in range(cx * cy):
        out_ref[pl.ds(c * nf, nf), :] = native_ref[pl.ds(c, nf, stride=cx * cy), :]


def to_columns(fields):
    nf, cx, cy, nz = fields.shape
    return pl.pallas_call(
        functools.partial(columns_kernel, cx, cy),
        out_shape=pltpu.VMEM((cx * cy * nf, nz), jnp.float32),
        in_specs=[VMEM],
        out_specs=VMEM,
        compiler_params=pltpu.CompilerParams(vmem_limit_bytes=2 * MIB),
        name="to_columns",
    )(fields.reshape(nf * cx * cy, nz))


def pack_kernel(cx, cy, nf, xa_ref, xb_ref, to_a_ref, to_b_ref):
    runs, size = corner_runs(min(cx, cy))
    even_s = lax.rem(lax.axis_index("sim"), 2) == 0
    even_l = lax.rem(lax.axis_index("learn"), 2) == 0

    def copy(s_is_even, l_is_even):
        for side, brick in enumerate((xa_ref, xb_ref)):
            is_east = s_is_even == (side == 0)
            for out_ref, north in ((to_a_ref, l_is_even), (to_b_ref, not l_is_even)):
                for d, count, first in runs:
                    x = d - 1 if is_east else cx - d
                    y = cy - count if north else 0
                    rows = brick[pl.ds((x * cy + y) * nf, count * nf), :]
                    out_ref[pl.ds((side * size + first) * nf, count * nf), :] = rows

    each_case(even_s, even_l, copy)


def pack_corners(xa, xb, cx, cy, nf):
    nz = xa.shape[1]
    size = 2 * corner_runs(min(cx, cy))[1]
    shape = pltpu.VMEM((size * nf, nz), jnp.float32)
    return pl.pallas_call(
        functools.partial(pack_kernel, cx, cy, nf),
        out_shape=(shape, shape),
        in_specs=[VMEM, VMEM],
        out_specs=(VMEM, VMEM),
        compiler_params=pltpu.CompilerParams(vmem_limit_bytes=MIB),
        name="pack_corners",
    )(*in_vmem(xa, xb))


def round_kernel(
    cx, cy, nf, steps, last, own_ref, xa_ref, xb_ref, ya_ref, yb_ref, ca_ref, cb_ref, dif_ref, sto_ref,
    state_ref, snap_ref, u_ref, m_ref, rate_ref,
):
    nz = own_ref.shape[1]
    reach = 2 * steps
    wide_x, wide_y = cx + 2 * reach, cy + 2 * reach
    s, l = lax.axis_index("sim"), lax.axis_index("learn")
    ns, nl = lax.axis_size("sim"), lax.axis_size("learn")
    even_s, even_l = lax.rem(s, 2) == 0, lax.rem(l, 2) == 0
    has_west, has_east = s > 0, s < ns - 1
    has_south, has_north = l > 0, l < nl - 1

    def place(ref, x0, y0):
        for i in range(cx):
            u_ref[pl.ds(((x0 + i) * wide_y + y0) * nf, cy * nf), :] = ref[pl.ds(i * cy * nf, cy * nf), :]

    def clear(x0, x1, y0, y1):
        zeros = jnp.zeros(((y1 - y0) * nf, nz), jnp.float32)

        def trip(x, carry):
            for ref in (u_ref, m_ref):
                ref[pl.ds(pl.multiple_of((x * wide_y + y0) * nf, nf), (y1 - y0) * nf), :] = zeros
            return carry

        lax.fori_loop(x0, x1, trip, 0)

    place(own_ref, reach, reach)
    runs, size = corner_runs(reach)

    def receive(s_is_even, l_is_even):
        for side, brick in enumerate((xa_ref, xb_ref)):
            is_east = s_is_even == (side == 0)

            @pl.when(has_east if is_east else has_west)
            def _(brick=brick, is_east=is_east):
                place(brick, reach + cx if is_east else 0, reach)

        for corner, brick, north in ((ca_ref, ya_ref, l_is_even), (cb_ref, yb_ref, not l_is_even)):

            @pl.when(has_north if north else has_south)
            def _(corner=corner, brick=brick, north=north):
                place(brick, reach, reach + cy if north else 0)
                for side in range(2):
                    is_east = s_is_even == (side == 0)
                    for d, count, first in runs:
                        x = reach + cx + d - 1 if is_east else reach - d
                        y = reach + cy if north else reach - count
                        rows = corner[pl.ds((side * size + first) * nf, count * nf), :]
                        u_ref[pl.ds((x * wide_y + y) * nf, count * nf), :] = rows

    each_case(even_s, even_l, receive)
    pl.when(jnp.logical_not(has_west))(lambda: clear(0, reach, 0, wide_y))
    pl.when(jnp.logical_not(has_east))(lambda: clear(reach + cx, wide_x, 0, wide_y))
    pl.when(jnp.logical_not(has_south))(lambda: clear(0, wide_x, 0, reach))
    pl.when(jnp.logical_not(has_north))(lambda: clear(0, wide_x, reach + cy, wide_y))

    field = lax.broadcasted_iota(jnp.int32, (nf, nz), 0)
    lane = lax.broadcasted_iota(jnp.int32, (nf, nz), 1)
    diffusivity, stoich = jnp.zeros((nf, nz), jnp.float32), jnp.zeros((nf, nz), jnp.float32)
    for f in range(nf):
        diffusivity = jnp.where(field == f, dif_ref[f], diffusivity)
        stoich = jnp.where(field == f, sto_ref[f], stoich)

    def coefficients(dt):
        return (
            1.0 * (dt / time_step) - 6.0 * dt * diffusivity,
            dt * (diffusivity - 0.5 * drift_x),
            dt * (diffusivity + 0.5 * drift_x),
            dt * (diffusivity - 0.5 * drift_y),
            dt * (diffusivity + 0.5 * drift_y),
            jnp.where(lane < nz - 1, dt * (diffusivity - 0.5 * drift_z), 0.0),
            jnp.where(lane > 0, dt * (diffusivity + 0.5 * drift_z), 0.0),
            dt * arrhenius * stoich,
        )

    in_south = jnp.where(has_south, 1.0, 0.0)
    in_north = jnp.where(has_north, 1.0, 0.0)

    def rows_block(src, dst, old, coefs, rows):
        cc, ce, cw, cn, cs, cu, cl, ck = coefs

        def load(x, y):
            return src[pl.ds((x * wide_y + y) * nf, nf), :]

        for k, (x, beyond) in enumerate(rows):
            y_first, width = reach - beyond, cy + 2 * beyond
            for p in range(0, width, nf):
                base = (x * wide_y + y_first + p) * nf
                u0 = src[pl.ds(base, nf, stride=nf), :]
                u1 = src[pl.ds(base + 1, nf, stride=nf), :]
                u7 = src[pl.ds(base + 7, nf, stride=nf), :]
                rate = jnp.tanh(u0) * jnp.tanh(u1) * jnp.exp(-activation / (1.0 + u7 * u7))
                rate_ref[pl.ds(k * (wide_y + nf) + p, nf), :] = rate
        for k, (x, beyond) in enumerate(rows):
            y_first, width = reach - beyond, cy + 2 * beyond
            south, centre = load(x, y_first - 1), load(x, y_first)
            for j in range(width):
                y = y_first + j
                north = load(x, y + 1)
                value = cc * centre + cn * north + cs * south
                value += ce * load(x + 1, y) + cw * load(x - 1, y)
                value += cu * pltpu.roll(centre, nz - 1, 1) + cl * pltpu.roll(centre, 1, 1)
                value += ck * rate_ref[pl.ds(k * (wide_y + nf) + j, nf, stride=0), :]
                if old is not None:
                    value += 0.5 * old[pl.ds((x * wide_y + y) * nf, nf), :]
                if y < reach:
                    value *= in_south
                if y >= reach + cy:
                    value *= in_north
                dst[pl.ds((x * wide_y + y) * nf, nf), :] = value
                south, centre = centre, north

    def stage(src, dst, old, r, coefs):
        group = 4

        def trip(i, carry):
            x0 = reach + i * group
            rows_block(src, dst, old, coefs, [(x0 + k, r) for k in range(group)])
            return carry

        lax.fori_loop(0, cx // group, trip, 0)
        if r:

            @pl.when(has_west)
            def _():
                rows_block(src, dst, old, coefs, [(reach - d, r - d) for d in range(1, r + 1)])

            @pl.when(has_east)
            def _():
                rows_block(src, dst, old, coefs, [(reach + cx - 1 + d, r - d) for d in range(1, r + 1)])

    whole, half = coefficients(time_step), coefficients(0.5 * time_step)
    for t in range(steps):
        r = reach - 1 - 2 * t
        stage(u_ref, m_ref, None, r, whole)
        stage(m_ref, u_ref, u_ref, r - 1, half)
        for x in range(cx):
            for f in range(nf):
                value = u_ref[pl.ds(((reach + x) * wide_y + reach) * nf + f, cy, stride=nf), :]
                snap_ref[f * cx + x, pl.ds(t * cy, cy), :] = value
                if last and t == steps - 1:
                    state_ref[pl.ds((f * cx + x) * cy, cy), :] = value
    if not last:
        for i in range(cx):
            rows = u_ref[pl.ds(((reach + i) * wide_y + reach) * nf, cy * nf), :]
            state_ref[pl.ds(i * cy * nf, cy * nf), :] = rows


def advance(bricks, corners, dif, sto, cx, cy, nf, steps, last):
    nz = bricks[0].shape[1]
    wide = (cx + 4 * steps) * (cy + 4 * steps)
    rows = max(cx, 2 * steps) * (cy + 4 * steps + nf)
    shape = (nf * cx * cy, nz)
    scalars = pl.BlockSpec(memory_space=pltpu.SMEM)
    return pl.pallas_call(
        functools.partial(round_kernel, cx, cy, nf, steps, last),
        out_shape=(
            jax.ShapeDtypeStruct(shape, jnp.float32) if last else pltpu.VMEM(shape, jnp.float32),
            pltpu.VMEM((nf * cx, steps * cy, nz), jnp.float32),
        ),
        in_specs=[VMEM] * 7 + [scalars] * 2,
        out_specs=(VMEM, VMEM),
        scratch_shapes=[
            pltpu.VMEM((wide * nf, nz), jnp.float32),
            pltpu.VMEM((wide * nf, nz), jnp.float32),
            pltpu.VMEM((rows, nz), jnp.float32),
        ],
        compiler_params=pltpu.CompilerParams(vmem_limit_bytes=8 * MIB),
        name="advance",
    )(*in_vmem(*bricks, *corners), dif, sto)


def split(value):
    high = value.astype(jnp.bfloat16)
    rest = value - high.astype(jnp.float32)
    middle = rest.astype(jnp.bfloat16)
    return high, middle, (rest - middle.astype(jnp.float32)).astype(jnp.bfloat16)


def project_kernel(cx, cy, steps, copies, basis_ref, snap_ref, *refs):
    earlier_ref, out_ref, acc_ref = refs if copies else (None, *refs)
    modes, nf, _, nz = basis_ref.shape
    pair = 2
    for g in range(nf // pair):
        total = None
        for p in range(cx // 2):
            left, right = [], []
            for f in range(g * pair, (g + 1) * pair):
                left.append(basis_ref[:, f, pl.ds(p * 2 * cy, 2 * cy), :].reshape(modes * 2 * cy, nz))
                rows = snap_ref[pl.ds(f * cx + 2 * p, 2)].reshape(2 * steps * cy, nz)
                right.append(rows.astype(jnp.bfloat16))
            term = lax.dot_general(
                jnp.concatenate(right, axis=1),
                jnp.concatenate(left, axis=1),
                (((1,), (1,)), ((), ())),
                preferred_element_type=jnp.float32,
            )
            total = term if total is None else total + term
        acc_ref[...] = total if g == 0 else acc_ref[...] + total

    lanes = 8 * 2 * cy
    blocks = modes * 2 * cy // lanes
    row = lax.broadcasted_iota(jnp.int32, (cy, lanes), 0)
    column = lax.broadcasted_iota(jnp.int32, (cy, lanes), 1)
    same_y = row == lax.rem(column, cy)
    first_x = lax.rem(column // cy, 2) == 0
    mode_of = lax.broadcasted_iota(jnp.int32, (lanes, modes), 0) // (2 * cy)
    mode = lax.broadcasted_iota(jnp.int32, (lanes, modes), 1)
    summed = None
    for k in range(blocks):
        kept = []
        for t in range(steps):
            west = acc_ref[pl.ds(t * cy, cy), pl.ds(k * lanes, lanes)]
            east = acc_ref[pl.ds((steps + t) * cy, cy), pl.ds(k * lanes, lanes)]
            kept.append(jnp.where(same_y, jnp.where(first_x, west, east), 0.0))
        gather = (mode - 8 * k == mode_of).astype(jnp.bfloat16)
        term = jnp.dot(
            jnp.concatenate(split(jnp.concatenate(kept, axis=0)), axis=0), gather, preferred_element_type=jnp.float32
        )
        summed = term if summed is None else summed + term
    count = steps * cy
    summed = summed[:count] + summed[count : 2 * count] + summed[2 * count :]
    result = jnp.sum(summed.reshape(steps, cy, modes), axis=1)
    if copies:
        both = jnp.concatenate([earlier_ref[...], result], axis=0)
        for n in range(copies):
            out_ref[n] = both
    else:
        out_ref[...] = result


def project(basis, snaps, cx, cy, steps, earlier=None, copies=0):
    modes = basis.shape[0]
    shape = (steps, modes)
    operands = in_vmem(snaps)
    if copies:
        shape = (copies, earlier.shape[0] + steps, modes)
        operands += in_vmem(earlier)
    return pl.pallas_call(
        functools.partial(project_kernel, cx, cy, steps, copies),
        out_shape=jax.ShapeDtypeStruct(shape, jnp.float32) if copies else pltpu.VMEM(shape, jnp.float32),
        in_specs=[VMEM] * (1 + len(operands)),
        out_specs=VMEM,
        scratch_shapes=[pltpu.VMEM((2 * steps * cy, modes * 2 * cy), jnp.float32)],
        compiler_params=pltpu.CompilerParams(vmem_limit_bytes=8 * MIB),
        name="project",
    )(basis, *operands)


def pair_tables(modes):
    upper_pairs = np.triu_indices(modes)
    first_table = np.concatenate([np.zeros(modes), upper_pairs[0] + 1]).astype(np.int32)
    second_table = np.concatenate([np.arange(modes) + 1, upper_pairs[1] + 1]).astype(np.int32)
    return (first_table, second_table)


def infer_kernel(shares_ref, gram_ref, picks_ref, reduced_ref, pod_ref, rhs_ref):
    steps, modes = reduced_ref.shape
    block = rhs_ref.shape[1]
    reduced = shares_ref[0]
    for n in range(1, shares_ref.shape[0]):
        reduced += shares_ref[n]
    reduced_ref[...] = reduced
    transposed = (((0,), (0,)), ((), ()))
    pod_ref[...] = gram_ref[...] + lax.dot_general(
        reduced, reduced, transposed, precision=lax.Precision.HIGHEST, preferred_element_type=jnp.float32
    )
    wide = picks_ref.shape[0]
    padded = jnp.concatenate([reduced, jnp.zeros((steps, wide - modes), jnp.float32)], axis=1)
    lane = lax.broadcasted_iota(jnp.int32, (steps, wide), 1)
    widened = jnp.where(lane == 0, 1.0, pltpu.roll(padded, 1, 1))
    picked = jnp.dot(jnp.concatenate(split(widened), axis=0), picks_ref[...], preferred_element_type=jnp.float32)
    picked = picked[:steps] + picked[steps : 2 * steps] + picked[2 * steps :]
    features = picked[:, :block] * picked[:, picks_ref.shape[1] // 2 :][:, :block]
    row = lax.broadcasted_iota(jnp.int32, (steps, modes), 0)
    changes = jnp.where(row < steps - 1, pltpu.roll(reduced, steps - 1, 0) - reduced, 0.0)
    ch, cm, cl = split(changes)
    fh, fm, fl = split(features)
    rhs_ref[...] = lax.dot_general(
        jnp.concatenate([ch, ch, cm, ch, cm, cl], axis=0),
        jnp.concatenate([fh, fm, fh, fl, fm, fh], axis=0),
        transposed,
        preferred_element_type=jnp.float32,
    )


def infer(shares, gram_old, nl):
    count, steps, modes = shares.shape
    tables = np.stack(pair_tables(modes))
    block = tables.shape[1] // nl
    lanes = -(-block // 128) * 128
    wide = -(-(modes + 1) // 128) * 128
    index = lax.dynamic_slice_in_dim(jnp.asarray(tables), lax.axis_index("learn") * block, block, axis=1)
    index = jnp.pad(index, ((0, 0), (0, lanes - block)), constant_values=-1).reshape(1, 2 * lanes)
    picks = (lax.broadcasted_iota(jnp.int32, (wide, 2 * lanes), 0) == index).astype(jnp.bfloat16)
    reduced, pod_gram, rhs = pl.pallas_call(
        infer_kernel,
        out_shape=(
            jax.ShapeDtypeStruct((steps, modes), jnp.float32),
            jax.ShapeDtypeStruct((modes, modes), jnp.float32),
            jax.ShapeDtypeStruct((modes, block), jnp.float32),
        ),
        in_specs=[VMEM] * 3,
        out_specs=(VMEM, VMEM, VMEM),
        compiler_params=pltpu.CompilerParams(vmem_limit_bytes=8 * MIB),
        name="infer",
    )(*in_vmem(shares, gram_old, picks))
    return reduced.T, pod_gram, rhs.T


def body(fields, diffusivity, stoich, basis, gram_old):
    nf, cx, cy, nz = fields.shape
    ns, nl = lax.axis_size("sim"), lax.axis_size("learn")
    steps = min(cx, cy) // 2
    rounds = STEPS // steps
    x_even, x_odd, y_even, y_odd, y_far = swaps(ns, nl)
    state = to_columns(fields)
    (basis,) = in_vmem(basis.reshape(basis.shape[0], nf, cx * cy, nz))
    share = None
    for n in range(rounds):
        ya = lax.ppermute(state, BOTH, y_even)
        yb = lax.ppermute(state, BOTH, y_odd)
        xa = lax.ppermute(state, BOTH, x_even)
        xb = lax.ppermute(state, BOTH, x_odd)
        if n:
            part = project(basis, snaps, cx, cy, steps)
            xa, xb, part = lax.optimization_barrier((xa, xb, part))
            share = part if share is None else jnp.concatenate([share, part], axis=0)
        to_a, to_b = pack_corners(xa, xb, cx, cy, nf)
        ca = lax.ppermute(to_a, BOTH, y_even)
        cb = lax.ppermute(to_b, BOTH, y_far)
        bricks = (state, xa, xb, ya, yb)
        state, snaps = advance(bricks, (ca, cb), diffusivity, stoich, cx, cy, nf, steps, n == rounds - 1)
    sent = project(basis, snaps, cx, cy, steps, share, ns * nl)
    shares = lax.all_to_all(sent, BOTH, 0, 0)
    reduced, pod_gram, rhs_block = infer(shares, gram_old, nl)
    return (state.reshape(fields.shape), reduced, pod_gram, rhs_block)


def solution(mesh):
    in_specs = (P(None, "sim", "learn", None), P(), P(), P(None, None, "sim", "learn", None), P())
    out_specs = (P(None, "sim", "learn", None), P(), P(), P("learn", None))
    return jax.shard_map(body, mesh=mesh, in_specs=in_specs, out_specs=out_specs, check_vma=False)
```

```python
import functools

import jax
import jax.numpy as jnp
import numpy as np
from jax import lax
from jax.experimental import pallas as pl
from jax.experimental.pallas import tpu as pltpu
from jax.sharding import PartitionSpec as P

STEPS = 8

time_step = 0.1
drift_x = 1.2
drift_y = 1.0
drift_z = 0.3
arrhenius = 2.0
activation = 1.0

BOTH = ("sim", "learn")
VMEM = pl.BlockSpec(memory_space=pltpu.VMEM)
SMEM = pl.BlockSpec(memory_space=pltpu.SMEM)
MIB = 1024 * 1024


def both_ways(pairs):
    return [(a, b) for a, b in pairs] + [(b, a) for a, b in pairs]


def swaps(ns, nl):
    x_even = both_ways([(s * nl + l, (s + 1) * nl + l) for s in range(0, ns, 2) for l in range(nl)])
    x_odd = [(s * nl + l, (s + 1) * nl + l) for s in range(1, ns - 1, 2) for l in range(nl)]
    x_odd += [(s * nl + l, s * nl + l + 1) for s in (0, ns - 1) for l in range(0, nl, 2)]
    y_even = both_ways([(s * nl + l, s * nl + l + 1) for s in range(ns) for l in range(0, nl, 2)])
    y_odd = [(s * nl + l, s * nl + l + 1) for s in range(ns) for l in range(1, nl - 1, 2)]
    y_far = y_odd + [(s * nl + l, (s + 1) * nl + l) for s in range(0, ns, 2) for l in (0, nl - 1)]
    y_odd = y_odd + [(s * nl, s * nl + nl - 1) for s in range(ns)]
    return x_even, both_ways(x_odd), y_even, both_ways(y_odd), both_ways(y_far)


def in_vmem(*arrays):
    return [pltpu.with_memory_space_constraint(a, pltpu.VMEM) for a in arrays]


def corner_runs(reach):
    runs, first = [], 0
    for d in range(1, reach):
        runs.append((d, reach - d, first))
        first += reach - d
    return runs, first


def each_case(first, second, body):
    for a in (True, False):
        for b in (True, False):

            @pl.when(jnp.logical_and(first == a, second == b))
            def _(a=a, b=b):
                body(a, b)


def columns_kernel(cx, cy, dif_ref, sto_ref, native_ref, out_ref, factors_ref):
    nf = native_ref.shape[0] // (cx * cy)
    field = lax.broadcasted_iota(jnp.int32, (nf, native_ref.shape[1]), 0)
    for n, ref in enumerate((dif_ref, sto_ref)):
        value = jnp.zeros(field.shape, jnp.float32)
        for f in range(nf):
            value = jnp.where(field == f, ref[f], value)
        factors_ref[n] = value
    for c in range(cx * cy):
        out_ref[pl.ds(c * nf, nf), :] = native_ref[pl.ds(c, nf, stride=cx * cy), :]


def to_columns(fields, diffusivity, stoich):
    nf, cx, cy, nz = fields.shape
    return pl.pallas_call(
        functools.partial(columns_kernel, cx, cy),
        out_shape=(pltpu.VMEM((cx * cy * nf, nz), jnp.float32), pltpu.VMEM((2, nf, nz), jnp.float32)),
        in_specs=[SMEM, SMEM, VMEM],
        out_specs=(VMEM, VMEM),
        compiler_params=pltpu.CompilerParams(vmem_limit_bytes=2 * MIB),
        name="to_columns",
    )(diffusivity, stoich, fields.reshape(nf * cx * cy, nz))


def pack_kernel(cx, cy, nf, xa_ref, xb_ref, to_a_ref, to_b_ref):
    runs, size = corner_runs(min(cx, cy))
    even_s = lax.rem(lax.axis_index("sim"), 2) == 0
    even_l = lax.rem(lax.axis_index("learn"), 2) == 0

    def copy(s_is_even, l_is_even):
        for side, brick in enumerate((xa_ref, xb_ref)):
            is_east = s_is_even == (side == 0)
            for out_ref, north in ((to_a_ref, l_is_even), (to_b_ref, not l_is_even)):
                for d, count, first in runs:
                    x = d - 1 if is_east else cx - d
                    y = cy - count if north else 0
                    rows = brick[pl.ds((x * cy + y) * nf, count * nf), :]
                    out_ref[pl.ds((side * size + first) * nf, count * nf), :] = rows

    each_case(even_s, even_l, copy)


def pack_corners(xa, xb, cx, cy, nf):
    nz = xa.shape[1]
    size = 2 * corner_runs(min(cx, cy))[1]
    shape = pltpu.VMEM((size * nf, nz), jnp.float32)
    return pl.pallas_call(
        functools.partial(pack_kernel, cx, cy, nf),
        out_shape=(shape, shape),
        in_specs=[VMEM, VMEM],
        out_specs=(VMEM, VMEM),
        compiler_params=pltpu.CompilerParams(vmem_limit_bytes=MIB),
        name="pack_corners",
    )(*in_vmem(xa, xb))


def round_kernel(
    cx, cy, nf, steps, last, own_ref, xa_ref, xb_ref, ya_ref, yb_ref, ca_ref, cb_ref, factors_ref,
    state_ref, snap_ref, u_ref, m_ref, rate_ref,
):
    nz = own_ref.shape[1]
    reach = 2 * steps
    wide_x, wide_y = cx + 2 * reach, cy + 2 * reach
    s, l = lax.axis_index("sim"), lax.axis_index("learn")
    ns, nl = lax.axis_size("sim"), lax.axis_size("learn")
    even_s, even_l = lax.rem(s, 2) == 0, lax.rem(l, 2) == 0
    has_west, has_east = s > 0, s < ns - 1
    has_south, has_north = l > 0, l < nl - 1

    def place(ref, x0, y0):
        for i in range(cx):
            u_ref[pl.ds(((x0 + i) * wide_y + y0) * nf, cy * nf), :] = ref[pl.ds(i * cy * nf, cy * nf), :]

    def clear(x0, x1, y0, y1):
        zeros = jnp.zeros(((y1 - y0) * nf, nz), jnp.float32)

        def trip(x, carry):
            for ref in (u_ref, m_ref):
                ref[pl.ds(pl.multiple_of((x * wide_y + y0) * nf, nf), (y1 - y0) * nf), :] = zeros
            return carry

        lax.fori_loop(x0, x1, trip, 0)

    place(own_ref, reach, reach)
    runs, size = corner_runs(reach)

    def receive(s_is_even, l_is_even):
        for side, brick in enumerate((xa_ref, xb_ref)):
            is_east = s_is_even == (side == 0)

            @pl.when(has_east if is_east else has_west)
            def _(brick=brick, is_east=is_east):
                place(brick, reach + cx if is_east else 0, reach)

        for corner, brick, north in ((ca_ref, ya_ref, l_is_even), (cb_ref, yb_ref, not l_is_even)):

            @pl.when(has_north if north else has_south)
            def _(corner=corner, brick=brick, north=north):
                place(brick, reach, reach + cy if north else 0)
                for side in range(2):
                    is_east = s_is_even == (side == 0)
                    for d, count, first in runs:
                        x = reach + cx + d - 1 if is_east else reach - d
                        y = reach + cy if north else reach - count
                        rows = corner[pl.ds((side * size + first) * nf, count * nf), :]
                        u_ref[pl.ds((x * wide_y + y) * nf, count * nf), :] = rows

    each_case(even_s, even_l, receive)
    pl.when(jnp.logical_not(has_west))(lambda: clear(0, reach, 0, wide_y))
    pl.when(jnp.logical_not(has_east))(lambda: clear(reach + cx, wide_x, 0, wide_y))
    pl.when(jnp.logical_not(has_south))(lambda: clear(0, wide_x, 0, reach))
    pl.when(jnp.logical_not(has_north))(lambda: clear(0, wide_x, reach + cy, wide_y))

    lane = lax.broadcasted_iota(jnp.int32, (nf, nz), 1)
    diffusivity, stoich = factors_ref[0], factors_ref[1]

    def coefficients(dt):
        return (
            1.0 * (dt / time_step) - 6.0 * dt * diffusivity,
            dt * (diffusivity - 0.5 * drift_x),
            dt * (diffusivity + 0.5 * drift_x),
            dt * (diffusivity - 0.5 * drift_y),
            dt * (diffusivity + 0.5 * drift_y),
            jnp.where(lane < nz - 1, dt * (diffusivity - 0.5 * drift_z), 0.0),
            jnp.where(lane > 0, dt * (diffusivity + 0.5 * drift_z), 0.0),
            dt * arrhenius * stoich,
        )

    in_south = jnp.where(has_south, 1.0, 0.0)
    in_north = jnp.where(has_north, 1.0, 0.0)

    def rows_block(src, dst, old, coefs, rows):
        cc, ce, cw, cn, cs, cu, cl, ck = coefs

        def load(x, y):
            return src[pl.ds((x * wide_y + y) * nf, nf), :]

        for k, (x, beyond) in enumerate(rows):
            y_first, width = reach - beyond, cy + 2 * beyond
            for p in range(0, width, nf):
                base = (x * wide_y + y_first + p) * nf
                u0 = src[pl.ds(base, nf, stride=nf), :]
                u1 = src[pl.ds(base + 1, nf, stride=nf), :]
                u7 = src[pl.ds(base + 7, nf, stride=nf), :]
                rate = jnp.tanh(u0) * jnp.tanh(u1) * jnp.exp(-activation / (1.0 + u7 * u7))
                rate_ref[pl.ds(k * (wide_y + nf) + p, nf), :] = rate
        for k, (x, beyond) in enumerate(rows):
            y_first, width = reach - beyond, cy + 2 * beyond
            south, centre = load(x, y_first - 1), load(x, y_first)
            for j in range(width):
                y = y_first + j
                north = load(x, y + 1)
                value = cc * centre + cn * north + cs * south
                value += ce * load(x + 1, y) + cw * load(x - 1, y)
                value += cu * pltpu.roll(centre, nz - 1, 1) + cl * pltpu.roll(centre, 1, 1)
                value += ck * rate_ref[pl.ds(k * (wide_y + nf) + j, nf, stride=0), :]
                if old is not None:
                    value += 0.5 * old[pl.ds((x * wide_y + y) * nf, nf), :]
                if y < reach:
                    value *= in_south
                if y >= reach + cy:
                    value *= in_north
                dst[pl.ds((x * wide_y + y) * nf, nf), :] = value
                south, centre = centre, north

    def stage(src, dst, old, r, coefs):
        group = 4

        def trip(i, carry):
            x0 = reach + i * group
            rows_block(src, dst, old, coefs, [(x0 + k, r) for k in range(group)])
            return carry

        lax.fori_loop(0, cx // group, trip, 0)
        if r:

            @pl.when(has_west)
            def _():
                rows_block(src, dst, old, coefs, [(reach - d, r - d) for d in range(1, r + 1)])

            @pl.when(has_east)
            def _():
                rows_block(src, dst, old, coefs, [(reach + cx - 1 + d, r - d) for d in range(1, r + 1)])

    whole, half = coefficients(time_step), coefficients(0.5 * time_step)
    for t in range(steps):
        r = reach - 1 - 2 * t
        stage(u_ref, m_ref, None, r, whole)
        stage(m_ref, u_ref, u_ref, r - 1, half)
        for x in range(cx):
            for f in range(nf):
                value = u_ref[pl.ds(((reach + x) * wide_y + reach) * nf + f, cy, stride=nf), :]
                snap_ref[f * cx + x, pl.ds(t * cy, cy), :] = value
                if last and t == steps - 1:
                    state_ref[pl.ds((f * cx + x) * cy, cy), :] = value
    if not last:
        for i in range(cx):
            rows = u_ref[pl.ds(((reach + i) * wide_y + reach) * nf, cy * nf), :]
            state_ref[pl.ds(i * cy * nf, cy * nf), :] = rows


def advance(bricks, corners, factors, cx, cy, nf, steps, last):
    nz = bricks[0].shape[1]
    wide = (cx + 4 * steps) * (cy + 4 * steps)
    rows = max(cx, 2 * steps) * (cy + 4 * steps + nf)
    shape = (nf * cx * cy, nz)
    return pl.pallas_call(
        functools.partial(round_kernel, cx, cy, nf, steps, last),
        out_shape=(
            pltpu.VMEM(shape, jnp.float32),
            pltpu.VMEM((nf * cx, steps * cy, nz), jnp.float32),
        ),
        in_specs=[VMEM] * 8,
        out_specs=(VMEM, VMEM),
        scratch_shapes=[
            pltpu.VMEM((wide * nf, nz), jnp.float32),
            pltpu.VMEM((wide * nf, nz), jnp.float32),
            pltpu.VMEM((rows, nz), jnp.float32),
        ],
        compiler_params=pltpu.CompilerParams(vmem_limit_bytes=8 * MIB),
        name="advance",
    )(*in_vmem(*bricks, *corners, factors))


def split(value):
    high = value.astype(jnp.bfloat16)
    rest = value - high.astype(jnp.float32)
    middle = rest.astype(jnp.bfloat16)
    return high, middle, (rest - middle.astype(jnp.float32)).astype(jnp.bfloat16)


def project_kernel(cx, cy, steps, copies, basis_ref, snap_ref, *refs):
    earlier_ref, out_ref, acc_ref = refs if copies else (None, *refs)
    modes, nf, _, nz = basis_ref.shape
    pair = 2
    for g in range(nf // pair):
        total = None
        for p in range(cx // 2):
            left, right = [], []
            for f in range(g * pair, (g + 1) * pair):
                left.append(basis_ref[:, f, pl.ds(p * 2 * cy, 2 * cy), :].reshape(modes * 2 * cy, nz))
                rows = snap_ref[pl.ds(f * cx + 2 * p, 2)].reshape(2 * steps * cy, nz)
                right.append(rows.astype(jnp.bfloat16))
            term = lax.dot_general(
                jnp.concatenate(right, axis=1),
                jnp.concatenate(left, axis=1),
                (((1,), (1,)), ((), ())),
                preferred_element_type=jnp.float32,
            )
            total = term if total is None else total + term
        acc_ref[...] = total if g == 0 else acc_ref[...] + total

    lanes = 8 * 2 * cy
    blocks = modes * 2 * cy // lanes
    row = lax.broadcasted_iota(jnp.int32, (cy, lanes), 0)
    column = lax.broadcasted_iota(jnp.int32, (cy, lanes), 1)
    same_y = row == lax.rem(column, cy)
    first_x = lax.rem(column // cy, 2) == 0
    mode_of = lax.broadcasted_iota(jnp.int32, (lanes, modes), 0) // (2 * cy)
    mode = lax.broadcasted_iota(jnp.int32, (lanes, modes), 1)
    summed = None
    for k in range(blocks):
        kept = []
        for t in range(steps):
            west = acc_ref[pl.ds(t * cy, cy), pl.ds(k * lanes, lanes)]
            east = acc_ref[pl.ds((steps + t) * cy, cy), pl.ds(k * lanes, lanes)]
            kept.append(jnp.where(same_y, jnp.where(first_x, west, east), 0.0))
        gather = (mode - 8 * k == mode_of).astype(jnp.bfloat16)
        term = jnp.dot(
            jnp.concatenate(split(jnp.concatenate(kept, axis=0)), axis=0), gather, preferred_element_type=jnp.float32
        )
        summed = term if summed is None else summed + term
    count = steps * cy
    summed = summed[:count] + summed[count : 2 * count] + summed[2 * count :]
    result = jnp.sum(summed.reshape(steps, cy, modes), axis=1)
    if copies:
        both = jnp.concatenate([earlier_ref[...], result], axis=0)
        for n in range(copies):
            out_ref[n] = both
    else:
        out_ref[...] = result


def project(basis, snaps, cx, cy, steps, earlier=None, copies=0):
    modes = basis.shape[0]
    shape = (steps, modes)
    operands = in_vmem(snaps)
    if copies:
        shape = (copies, earlier.shape[0] + steps, modes)
        operands += in_vmem(earlier)
    return pl.pallas_call(
        functools.partial(project_kernel, cx, cy, steps, copies),
        out_shape=jax.ShapeDtypeStruct(shape, jnp.float32) if copies else pltpu.VMEM(shape, jnp.float32),
        in_specs=[VMEM] * (1 + len(operands)),
        out_specs=VMEM,
        scratch_shapes=[pltpu.VMEM((2 * steps * cy, modes * 2 * cy), jnp.float32)],
        compiler_params=pltpu.CompilerParams(vmem_limit_bytes=8 * MIB),
        name="project",
    )(basis, *operands)


def pair_tables(modes):
    upper_pairs = np.triu_indices(modes)
    first_table = np.concatenate([np.zeros(modes), upper_pairs[0] + 1]).astype(np.int32)
    second_table = np.concatenate([np.arange(modes) + 1, upper_pairs[1] + 1]).astype(np.int32)
    return (first_table, second_table)


def infer_kernel(shares_ref, gram_ref, picks_ref, reduced_ref, pod_ref, rhs_ref):
    steps, modes = reduced_ref.shape
    block = rhs_ref.shape[1]
    reduced = shares_ref[0]
    for n in range(1, shares_ref.shape[0]):
        reduced += shares_ref[n]
    reduced_ref[...] = reduced
    transposed = (((0,), (0,)), ((), ()))
    pod_ref[...] = gram_ref[...] + lax.dot_general(
        reduced, reduced, transposed, precision=lax.Precision.HIGHEST, preferred_element_type=jnp.float32
    )
    wide = picks_ref.shape[0]
    padded = jnp.concatenate([reduced, jnp.zeros((steps, wide - modes), jnp.float32)], axis=1)
    lane = lax.broadcasted_iota(jnp.int32, (steps, wide), 1)
    widened = jnp.where(lane == 0, 1.0, pltpu.roll(padded, 1, 1))
    picked = jnp.dot(jnp.concatenate(split(widened), axis=0), picks_ref[...], preferred_element_type=jnp.float32)
    picked = picked[:steps] + picked[steps : 2 * steps] + picked[2 * steps :]
    features = picked[:, :block] * picked[:, picks_ref.shape[1] // 2 :][:, :block]
    row = lax.broadcasted_iota(jnp.int32, (steps, modes), 0)
    changes = jnp.where(row < steps - 1, pltpu.roll(reduced, steps - 1, 0) - reduced, 0.0)
    ch, cm, cl = split(changes)
    fh, fm, fl = split(features)
    rhs_ref[...] = lax.dot_general(
        jnp.concatenate([ch, ch, cm, ch, cm, cl], axis=0),
        jnp.concatenate([fh, fm, fh, fl, fm, fh], axis=0),
        transposed,
        preferred_element_type=jnp.float32,
    )


def picks_kernel(tables_ref, after_ref, out_ref):
    del after_ref
    index = tables_ref[pl.ds(lax.axis_index("learn"), 1), :]
    place = lax.broadcasted_iota(jnp.int32, out_ref.shape, 0)
    out_ref[...] = jnp.where(place == index, 1.0, 0.0).astype(jnp.bfloat16)


def pick_matrices(modes, nl, after):
    tables = np.stack(pair_tables(modes))
    block = tables.shape[1] // nl
    lanes = -(-block // 128) * 128
    tables = tables.reshape(2, nl, block).transpose(1, 0, 2)
    tables = np.pad(tables, ((0, 0), (0, 0), (0, lanes - block)), constant_values=-1).reshape(nl, 2 * lanes)
    wide = -(-(modes + 1) // 128) * 128
    return block, pl.pallas_call(
        picks_kernel,
        out_shape=pltpu.VMEM((wide, 2 * lanes), jnp.bfloat16),
        in_specs=[VMEM, pl.BlockSpec(memory_space=pl.ANY)],
        out_specs=VMEM,
        compiler_params=pltpu.CompilerParams(vmem_limit_bytes=4 * MIB),
        name="pick_matrices",
    )(jnp.asarray(tables), after)


def infer(shares, gram_old, picks, block):
    count, steps, modes = shares.shape
    reduced, pod_gram, rhs = pl.pallas_call(
        infer_kernel,
        out_shape=(
            jax.ShapeDtypeStruct((steps, modes), jnp.float32),
            jax.ShapeDtypeStruct((modes, modes), jnp.float32),
            jax.ShapeDtypeStruct((modes, block), jnp.float32),
        ),
        in_specs=[VMEM] * 3,
        out_specs=(VMEM, VMEM, VMEM),
        compiler_params=pltpu.CompilerParams(vmem_limit_bytes=8 * MIB),
        name="infer",
    )(*in_vmem(shares, gram_old, picks))
    return reduced.T, pod_gram, rhs.T


def body(fields, diffusivity, stoich, basis, gram_old):
    nf, cx, cy, nz = fields.shape
    ns, nl = lax.axis_size("sim"), lax.axis_size("learn")
    steps = min(cx, cy) // 2
    rounds = STEPS // steps
    x_even, x_odd, y_even, y_odd, y_far = swaps(ns, nl)
    state, factors = to_columns(fields, diffusivity, stoich)
    (basis,) = in_vmem(basis.reshape(basis.shape[0], nf, cx * cy, nz))
    share = None
    for n in range(rounds):
        ya = lax.ppermute(state, BOTH, y_even)
        yb = lax.ppermute(state, BOTH, y_odd)
        xa = lax.ppermute(state, BOTH, x_even)
        xb = lax.ppermute(state, BOTH, x_odd)
        if n:
            part = project(basis, snaps, cx, cy, steps)
            xa, xb, part = lax.optimization_barrier((xa, xb, part))
            share = part if share is None else jnp.concatenate([share, part], axis=0)
        to_a, to_b = pack_corners(xa, xb, cx, cy, nf)
        ca = lax.ppermute(to_a, BOTH, y_even)
        cb = lax.ppermute(to_b, BOTH, y_far)
        bricks = (state, xa, xb, ya, yb)
        state, snaps = advance(bricks, (ca, cb), factors, cx, cy, nf, steps, n == rounds - 1)
    sent = project(basis, snaps, cx, cy, steps, share, ns * nl)
    shares = lax.all_to_all(sent, BOTH, 0, 0)
    block, picks = pick_matrices(gram_old.shape[0], nl, sent)
    reduced, pod_gram, rhs_block = infer(shares, gram_old, picks, block)
    return (state.reshape(fields.shape), reduced, pod_gram, rhs_block)


def solution(mesh):
    in_specs = (P(None, "sim", "learn", None), P(), P(), P(None, None, "sim", "learn", None), P())
    out_specs = (P(None, "sim", "learn", None), P(), P(), P("learn", None))
    return jax.shard_map(body, mesh=mesh, in_specs=in_specs, out_specs=out_specs, check_vma=False)
```

```python
import functools

import jax
import jax.numpy as jnp
import numpy as np
from jax import lax
from jax.experimental import pallas as pl
from jax.experimental.pallas import tpu as pltpu
from jax.sharding import PartitionSpec as P

STEPS = 8

time_step = 0.1
drift_x = 1.2
drift_y = 1.0
drift_z = 0.3
arrhenius = 2.0
activation = 1.0

BOTH = ("sim", "learn")
VMEM = pl.BlockSpec(memory_space=pltpu.VMEM)
SMEM = pl.BlockSpec(memory_space=pltpu.SMEM)
MIB = 1024 * 1024


def both_ways(pairs):
    return [(a, b) for a, b in pairs] + [(b, a) for a, b in pairs]


def swaps(ns, nl):
    x_even = both_ways([(s * nl + l, (s + 1) * nl + l) for s in range(0, ns, 2) for l in range(nl)])
    x_odd = [(s * nl + l, (s + 1) * nl + l) for s in range(1, ns - 1, 2) for l in range(nl)]
    x_odd += [(s * nl + l, s * nl + l + 1) for s in (0, ns - 1) for l in range(0, nl, 2)]
    y_even = both_ways([(s * nl + l, s * nl + l + 1) for s in range(ns) for l in range(0, nl, 2)])
    y_odd = [(s * nl + l, s * nl + l + 1) for s in range(ns) for l in range(1, nl - 1, 2)]
    far = 2 if ns % 4 == 0 else 1
    y_odd += [(s * nl + l, (s + far) * nl + l) for s in range(ns) if s // far % 2 == 0 for l in (0, nl - 1)]
    return x_even, both_ways(x_odd), y_even, both_ways(y_odd)


def in_vmem(*arrays):
    return [pltpu.with_memory_space_constraint(a, pltpu.VMEM) for a in arrays]


def corner_runs(reach):
    runs, first = [], 0
    for d in range(1, reach):
        runs.append((d, reach - d, first))
        first += reach - d
    return runs, first


def x_runs(reach, cy):
    parts, sizes = ([], []), [0, 0]
    for d in range(1, reach + 1):
        count = min(reach - d, cy)
        if 2 * count >= cy:
            cuts = ((0, 0, cy),)
        else:
            cuts = ((0, 0, count), (1, count, cy - count), (0, cy - count, cy))
        for part, low, high in cuts:
            if high > low:
                parts[part].append((d, low, high - low, sizes[part]))
                sizes[part] += high - low
    return parts, sizes


def in_first_part(reach, cy, d, y):
    for e, low, count, first in x_runs(reach, cy)[0][0]:
        if e == d and low <= y < low + count:
            return first + y - low
    raise ValueError((d, y))


def each_case(cond, body):
    pl.when(cond)(lambda: body(True))
    pl.when(jnp.logical_not(cond))(lambda: body(False))


def cut_bricks(cx, cy, nf, load, a1_ref, b1_ref, a2_ref, b2_ref):
    parts, _ = x_runs(cx, cy)

    def cut(s_is_even):
        for part, a_ref, b_ref in ((0, a1_ref, b1_ref), (1, a2_ref, b2_ref)):
            for out_ref, is_east in ((a_ref, s_is_even), (b_ref, not s_is_even)):
                for d, y, count, first in parts[part]:
                    out_ref[pl.ds(first * nf, count * nf), :] = load(cx - d if is_east else d - 1, y, count)

    each_case(lax.rem(lax.axis_index("sim"), 2) == 0, cut)


def cut_shapes(cx, cy, nf, nz):
    sizes = x_runs(cx, cy)[1]
    return [pltpu.VMEM((size * nf, nz), jnp.float32) for size in (sizes[0], sizes[0], sizes[1], sizes[1])]


def columns_kernel(cx, cy, native_ref, out_ref, *cut_refs):
    nf = native_ref.shape[0] // (cx * cy)
    for c in range(cx * cy):
        out_ref[pl.ds(c * nf, nf), :] = native_ref[pl.ds(c, nf, stride=cx * cy), :]
    cut_bricks(cx, cy, nf, lambda x, y, n: out_ref[pl.ds((x * cy + y) * nf, n * nf), :], *cut_refs)


def to_columns(fields):
    nf, cx, cy, nz = fields.shape
    return pl.pallas_call(
        functools.partial(columns_kernel, cx, cy),
        out_shape=[pltpu.VMEM((cx * cy * nf, nz), jnp.float32), *cut_shapes(cx, cy, nf, nz)],
        in_specs=[VMEM],
        out_specs=[VMEM] * 5,
        compiler_params=pltpu.CompilerParams(vmem_limit_bytes=2 * MIB),
        name="to_columns",
    )(*in_vmem(fields.reshape(nf * cx * cy, nz)))


def factors_kernel(dif_ref, sto_ref, after_ref, out_ref):
    del after_ref
    _, nf, nz = out_ref.shape
    field = lax.broadcasted_iota(jnp.int32, (nf, nz), 0)
    for n, ref in enumerate((dif_ref, sto_ref)):
        value = jnp.zeros((nf, nz), jnp.float32)
        for f in range(nf):
            value = jnp.where(field == f, ref[f], value)
        out_ref[n] = value


def field_factors(diffusivity, stoich, nz, after):
    return pl.pallas_call(
        factors_kernel,
        out_shape=pltpu.VMEM((2, diffusivity.shape[0], nz), jnp.float32),
        in_specs=[SMEM, SMEM, pl.BlockSpec(memory_space=pl.ANY)],
        out_specs=VMEM,
        compiler_params=pltpu.CompilerParams(vmem_limit_bytes=MIB),
        name="field_factors",
    )(diffusivity, stoich, after)


def pack_kernel(cx, cy, nf, own_ref, xa_ref, xb_ref, to_a_ref, to_b_ref):
    runs, size = corner_runs(cx)

    def copy(l_is_even):
        for out_ref, north in ((to_a_ref, l_is_even), (to_b_ref, not l_is_even)):
            for side, brick in enumerate((xa_ref, xb_ref)):
                for d, count, first in runs:
                    row = in_first_part(cx, cy, d, cy - count if north else 0)
                    rows = brick[pl.ds(row * nf, count * nf), :]
                    out_ref[pl.ds((side * size + first) * nf, count * nf), :] = rows

    each_case(lax.rem(lax.axis_index("learn"), 2) == 0, copy)
    for x in range(cx):
        rows = own_ref[pl.ds(x * cy * nf, cy * nf), :]
        for out_ref in (to_a_ref, to_b_ref):
            out_ref[pl.ds((2 * size + x * cy) * nf, cy * nf), :] = rows


def pack_for_y(own, xa, xb, cx, cy, nf):
    nz = own.shape[1]
    size = 2 * corner_runs(cx)[1] + cx * cy
    shape = pltpu.VMEM((size * nf, nz), jnp.float32)
    return pl.pallas_call(
        functools.partial(pack_kernel, cx, cy, nf),
        out_shape=(shape, shape),
        in_specs=[VMEM] * 3,
        out_specs=(VMEM, VMEM),
        compiler_params=pltpu.CompilerParams(vmem_limit_bytes=MIB),
        name="pack_for_y",
    )(*in_vmem(own, xa, xb))


def round_kernel(
    cx, cy, nf, steps, last, own_ref, a1_ref, b1_ref, a2_ref, b2_ref, ya_ref, yb_ref, factors_ref,
    state_ref, snap_ref, *refs,
):
    cut_refs, (u_ref, m_ref, rate_ref) = refs[:-3], refs[-3:]
    nz = own_ref.shape[1]
    reach = 2 * steps
    wide_x, wide_y = cx + 2 * reach, cy + 2 * reach
    s, l = lax.axis_index("sim"), lax.axis_index("learn")
    ns, nl = lax.axis_size("sim"), lax.axis_size("learn")
    even_s, even_l = lax.rem(s, 2) == 0, lax.rem(l, 2) == 0
    has_west, has_east = s > 0, s < ns - 1
    has_south, has_north = l > 0, l < nl - 1

    def place(ref, row, x0, y0):
        for i in range(cx):
            rows = ref[pl.ds((row + i * cy) * nf, cy * nf), :]
            u_ref[pl.ds(((x0 + i) * wide_y + y0) * nf, cy * nf), :] = rows

    def halo_x(is_east, d):
        return reach + cx + d - 1 if is_east else reach - d

    def clear(x0, x1, y0, y1):
        zeros = jnp.zeros(((y1 - y0) * nf, nz), jnp.float32)

        def trip(x, carry):
            for ref in (u_ref, m_ref):
                ref[pl.ds(pl.multiple_of((x * wide_y + y0) * nf, nf), (y1 - y0) * nf), :] = zeros
            return carry

        lax.fori_loop(x0, x1, trip, 0)

    place(own_ref, 0, reach, reach)
    corners, size = corner_runs(reach)
    parts, _ = x_runs(reach, cy)

    def receive_x(s_is_even):
        for first_ref, rest_ref, is_east in ((a1_ref, a2_ref, s_is_even), (b1_ref, b2_ref, not s_is_even)):

            @pl.when(has_east if is_east else has_west)
            def _(first_ref=first_ref, rest_ref=rest_ref, is_east=is_east):
                for ref, runs in ((first_ref, parts[0]), (rest_ref, parts[1])):
                    for d, y, count, first in runs:
                        rows = ref[pl.ds(first * nf, count * nf), :]
                        u_ref[pl.ds((halo_x(is_east, d) * wide_y + reach + y) * nf, count * nf), :] = rows

    def receive_y(l_is_even):
        for ref, north in ((ya_ref, l_is_even), (yb_ref, not l_is_even)):

            @pl.when(has_north if north else has_south)
            def _(ref=ref, north=north):
                place(ref, 2 * size, reach, reach + cy if north else 0)

                def receive_corners(s_is_even):
                    for side in range(2):
                        for d, count, first in corners:
                            x = halo_x(s_is_even == (side == 0), d)
                            y = reach + cy if north else reach - count
                            rows = ref[pl.ds((side * size + first) * nf, count * nf), :]
                            u_ref[pl.ds((x * wide_y + y) * nf, count * nf), :] = rows

                each_case(even_s, receive_corners)

    each_case(even_s, receive_x)
    each_case(even_l, receive_y)
    pl.when(jnp.logical_not(has_west))(lambda: clear(0, reach, 0, wide_y))
    pl.when(jnp.logical_not(has_east))(lambda: clear(reach + cx, wide_x, 0, wide_y))
    pl.when(jnp.logical_not(has_south))(lambda: clear(0, wide_x, 0, reach))
    pl.when(jnp.logical_not(has_north))(lambda: clear(0, wide_x, reach + cy, wide_y))

    lane = lax.broadcasted_iota(jnp.int32, (nf, nz), 1)
    diffusivity, stoich = factors_ref[0], factors_ref[1]

    def coefficients(dt):
        return (
            1.0 * (dt / time_step) - 6.0 * dt * diffusivity,
            dt * (diffusivity - 0.5 * drift_x),
            dt * (diffusivity + 0.5 * drift_x),
            dt * (diffusivity - 0.5 * drift_y),
            dt * (diffusivity + 0.5 * drift_y),
            jnp.where(lane < nz - 1, dt * (diffusivity - 0.5 * drift_z), 0.0),
            jnp.where(lane > 0, dt * (diffusivity + 0.5 * drift_z), 0.0),
            dt * arrhenius * stoich,
        )

    in_south = jnp.where(has_south, 1.0, 0.0)
    in_north = jnp.where(has_north, 1.0, 0.0)

    def rows_block(src, dst, old, coefs, rows):
        cc, ce, cw, cn, cs, cu, cl, ck = coefs

        def load(x, y):
            return src[pl.ds((x * wide_y + y) * nf, nf), :]

        for k, (x, beyond) in enumerate(rows):
            y_first, width = reach - beyond, cy + 2 * beyond
            for p in range(0, width, nf):
                base = (x * wide_y + y_first + p) * nf
                u0 = src[pl.ds(base, nf, stride=nf), :]
                u1 = src[pl.ds(base + 1, nf, stride=nf), :]
                u7 = src[pl.ds(base + 7, nf, stride=nf), :]
                rate = jnp.tanh(u0) * jnp.tanh(u1) * jnp.exp(-activation / (1.0 + u7 * u7))
                rate_ref[pl.ds(k * (wide_y + nf) + p, nf), :] = rate
        for k, (x, beyond) in enumerate(rows):
            y_first, width = reach - beyond, cy + 2 * beyond
            south, centre = load(x, y_first - 1), load(x, y_first)
            for j in range(width):
                y = y_first + j
                north = load(x, y + 1)
                value = cc * centre + cn * north + cs * south
                value += ce * load(x + 1, y) + cw * load(x - 1, y)
                value += cu * pltpu.roll(centre, nz - 1, 1) + cl * pltpu.roll(centre, 1, 1)
                value += ck * rate_ref[pl.ds(k * (wide_y + nf) + j, nf, stride=0), :]
                if old is not None:
                    value += 0.5 * old[pl.ds((x * wide_y + y) * nf, nf), :]
                if y < reach:
                    value *= in_south
                if y >= reach + cy:
                    value *= in_north
                dst[pl.ds((x * wide_y + y) * nf, nf), :] = value
                south, centre = centre, north

    def stage(src, dst, old, r, coefs):
        group = 4

        def trip(i, carry):
            x0 = reach + i * group
            rows_block(src, dst, old, coefs, [(x0 + k, r) for k in range(group)])
            return carry

        lax.fori_loop(0, cx // group, trip, 0)
        if r:

            @pl.when(has_west)
            def _():
                rows_block(src, dst, old, coefs, [(reach - d, r - d) for d in range(1, r + 1)])

            @pl.when(has_east)
            def _():
                rows_block(src, dst, old, coefs, [(reach + cx - 1 + d, r - d) for d in range(1, r + 1)])

    whole, half = coefficients(time_step), coefficients(0.5 * time_step)
    for t in range(steps):
        r = reach - 1 - 2 * t
        stage(u_ref, m_ref, None, r, whole)
        stage(m_ref, u_ref, u_ref, r - 1, half)
        for x in range(cx):
            for f in range(nf):
                value = u_ref[pl.ds(((reach + x) * wide_y + reach) * nf + f, cy, stride=nf), :]
                snap_ref[f * cx + x, pl.ds(t * cy, cy), :] = value
                if last and t == steps - 1:
                    state_ref[pl.ds((f * cx + x) * cy, cy), :] = value
    if not last:
        for i in range(cx):
            rows = u_ref[pl.ds(((reach + i) * wide_y + reach) * nf, cy * nf), :]
            state_ref[pl.ds(i * cy * nf, cy * nf), :] = rows

        def brick(x, y, count):
            return u_ref[pl.ds(((reach + x) * wide_y + reach + y) * nf, count * nf), :]

        cut_bricks(cx, cy, nf, brick, *cut_refs)


def advance(operands, cx, cy, nf, steps, last):
    nz = operands[0].shape[1]
    wide = (cx + 4 * steps) * (cy + 4 * steps)
    rows = max(cx, 2 * steps) * (cy + 4 * steps + nf)
    shape = (nf * cx * cy, nz)
    cuts = [] if last else cut_shapes(cx, cy, nf, nz)
    return pl.pallas_call(
        functools.partial(round_kernel, cx, cy, nf, steps, last),
        out_shape=[
            pltpu.VMEM(shape, jnp.float32),
            pltpu.VMEM((nf * cx, steps * cy, nz), jnp.float32),
            *cuts,
        ],
        in_specs=[VMEM] * 8,
        out_specs=[VMEM] * (2 + len(cuts)),
        scratch_shapes=[
            pltpu.VMEM((wide * nf, nz), jnp.float32),
            pltpu.VMEM((wide * nf, nz), jnp.float32),
            pltpu.VMEM((rows, nz), jnp.float32),
        ],
        compiler_params=pltpu.CompilerParams(vmem_limit_bytes=8 * MIB),
        name="advance",
    )(*in_vmem(*operands))


def split(value):
    high = value.astype(jnp.bfloat16)
    rest = value - high.astype(jnp.float32)
    middle = rest.astype(jnp.bfloat16)
    return high, middle, (rest - middle.astype(jnp.float32)).astype(jnp.bfloat16)


def project_kernel(cx, cy, steps, copies, basis_ref, snap_ref, *refs):
    earlier_ref, out_ref, acc_ref = refs if copies else (None, *refs)
    modes, nf, _, nz = basis_ref.shape
    pair = 2
    for g in range(nf // pair):
        total = None
        for p in range(cx // 2):
            left, right = [], []
            for f in range(g * pair, (g + 1) * pair):
                left.append(basis_ref[:, f, pl.ds(p * 2 * cy, 2 * cy), :].reshape(modes * 2 * cy, nz))
                rows = snap_ref[pl.ds(f * cx + 2 * p, 2)].reshape(2 * steps * cy, nz)
                right.append(rows.astype(jnp.bfloat16))
            term = lax.dot_general(
                jnp.concatenate(right, axis=1),
                jnp.concatenate(left, axis=1),
                (((1,), (1,)), ((), ())),
                preferred_element_type=jnp.float32,
            )
            total = term if total is None else total + term
        acc_ref[...] = total if g == 0 else acc_ref[...] + total

    lanes = 8 * 2 * cy
    blocks = modes * 2 * cy // lanes
    row = lax.broadcasted_iota(jnp.int32, (cy, lanes), 0)
    column = lax.broadcasted_iota(jnp.int32, (cy, lanes), 1)
    same_y = row == lax.rem(column, cy)
    first_x = lax.rem(column // cy, 2) == 0
    mode_of = lax.broadcasted_iota(jnp.int32, (lanes, modes), 0) // (2 * cy)
    mode = lax.broadcasted_iota(jnp.int32, (lanes, modes), 1)
    summed = None
    for k in range(blocks):
        kept = []
        for t in range(steps):
            west = acc_ref[pl.ds(t * cy, cy), pl.ds(k * lanes, lanes)]
            east = acc_ref[pl.ds((steps + t) * cy, cy), pl.ds(k * lanes, lanes)]
            kept.append(jnp.where(same_y, jnp.where(first_x, west, east), 0.0))
        gather = (mode - 8 * k == mode_of).astype(jnp.bfloat16)
        term = jnp.dot(
            jnp.concatenate(split(jnp.concatenate(kept, axis=0)), axis=0), gather, preferred_element_type=jnp.float32
        )
        summed = term if summed is None else summed + term
    count = steps * cy
    summed = summed[:count] + summed[count : 2 * count] + summed[2 * count :]
    result = jnp.sum(summed.reshape(steps, cy, modes), axis=1)
    if copies:
        both = jnp.concatenate([earlier_ref[...], result], axis=0)
        for n in range(copies):
            out_ref[n] = both
    else:
        out_ref[...] = result


def project(basis, snaps, cx, cy, steps, earlier=None, copies=0):
    modes = basis.shape[0]
    shape = (steps, modes)
    operands = in_vmem(snaps)
    if copies:
        shape = (copies, earlier.shape[0] + steps, modes)
        operands += in_vmem(earlier)
    return pl.pallas_call(
        functools.partial(project_kernel, cx, cy, steps, copies),
        out_shape=jax.ShapeDtypeStruct(shape, jnp.float32) if copies else pltpu.VMEM(shape, jnp.float32),
        in_specs=[VMEM] * (1 + len(operands)),
        out_specs=VMEM,
        scratch_shapes=[pltpu.VMEM((2 * steps * cy, modes * 2 * cy), jnp.float32)],
        compiler_params=pltpu.CompilerParams(vmem_limit_bytes=8 * MIB),
        name="project",
    )(basis, *operands)


def pair_tables(modes):
    upper_pairs = np.triu_indices(modes)
    first_table = np.concatenate([np.zeros(modes), upper_pairs[0] + 1]).astype(np.int32)
    second_table = np.concatenate([np.arange(modes) + 1, upper_pairs[1] + 1]).astype(np.int32)
    return (first_table, second_table)


def infer_kernel(shares_ref, gram_ref, picks_ref, reduced_ref, pod_ref, rhs_ref):
    steps, modes = reduced_ref.shape
    block = rhs_ref.shape[1]
    reduced = shares_ref[0]
    for n in range(1, shares_ref.shape[0]):
        reduced += shares_ref[n]
    reduced_ref[...] = reduced
    transposed = (((0,), (0,)), ((), ()))
    pod_ref[...] = gram_ref[...] + lax.dot_general(
        reduced, reduced, transposed, precision=lax.Precision.HIGHEST, preferred_element_type=jnp.float32
    )
    wide = picks_ref.shape[0]
    padded = jnp.concatenate([reduced, jnp.zeros((steps, wide - modes), jnp.float32)], axis=1)
    lane = lax.broadcasted_iota(jnp.int32, (steps, wide), 1)
    widened = jnp.where(lane == 0, 1.0, pltpu.roll(padded, 1, 1))
    picked = jnp.dot(jnp.concatenate(split(widened), axis=0), picks_ref[...], preferred_element_type=jnp.float32)
    picked = picked[:steps] + picked[steps : 2 * steps] + picked[2 * steps :]
    features = picked[:, :block] * picked[:, picks_ref.shape[1] // 2 :][:, :block]
    row = lax.broadcasted_iota(jnp.int32, (steps, modes), 0)
    changes = jnp.where(row < steps - 1, pltpu.roll(reduced, steps - 1, 0) - reduced, 0.0)
    ch, cm, cl = split(changes)
    fh, fm, fl = split(features)
    rhs_ref[...] = lax.dot_general(
        jnp.concatenate([ch, ch, cm, ch, cm, cl], axis=0),
        jnp.concatenate([fh, fm, fh, fl, fm, fh], axis=0),
        transposed,
        preferred_element_type=jnp.float32,
    )


def picks_kernel(tables_ref, after_ref, out_ref):
    del after_ref
    index = tables_ref[pl.ds(lax.axis_index("learn"), 1), :]
    place = lax.broadcasted_iota(jnp.int32, out_ref.shape, 0)
    out_ref[...] = jnp.where(place == index, 1.0, 0.0).astype(jnp.bfloat16)


def pick_matrices(modes, nl, after):
    tables = np.stack(pair_tables(modes))
    block = tables.shape[1] // nl
    lanes = -(-block // 128) * 128
    tables = tables.reshape(2, nl, block).transpose(1, 0, 2)
    tables = np.pad(tables, ((0, 0), (0, 0), (0, lanes - block)), constant_values=-1).reshape(nl, 2 * lanes)
    wide = -(-(modes + 1) // 128) * 128
    return block, pl.pallas_call(
        picks_kernel,
        out_shape=pltpu.VMEM((wide, 2 * lanes), jnp.bfloat16),
        in_specs=[VMEM, pl.BlockSpec(memory_space=pl.ANY)],
        out_specs=VMEM,
        compiler_params=pltpu.CompilerParams(vmem_limit_bytes=4 * MIB),
        name="pick_matrices",
    )(jnp.asarray(tables), after)


def infer(shares, gram_old, picks, block):
    count, steps, modes = shares.shape
    reduced, pod_gram, rhs = pl.pallas_call(
        infer_kernel,
        out_shape=(
            jax.ShapeDtypeStruct((steps, modes), jnp.float32),
            jax.ShapeDtypeStruct((modes, modes), jnp.float32),
            jax.ShapeDtypeStruct((modes, block), jnp.float32),
        ),
        in_specs=[VMEM] * 3,
        out_specs=(VMEM, VMEM, VMEM),
        compiler_params=pltpu.CompilerParams(vmem_limit_bytes=8 * MIB),
        name="infer",
    )(*in_vmem(shares, gram_old, picks))
    return reduced.T, pod_gram, rhs.T


def body(fields, diffusivity, stoich, basis, gram_old):
    nf, cx, cy, nz = fields.shape
    ns, nl = lax.axis_size("sim"), lax.axis_size("learn")
    steps = min(cx, cy) // 2
    rounds = STEPS // steps
    x_even, x_odd, y_even, y_odd = swaps(ns, nl)
    state, *cuts = to_columns(fields)
    factors = field_factors(diffusivity, stoich, nz, state)
    (basis,) = in_vmem(basis.reshape(basis.shape[0], nf, cx * cy, nz))
    share = None
    for n in range(rounds):
        a1 = lax.ppermute(cuts[0], BOTH, x_even)
        b1 = lax.ppermute(cuts[1], BOTH, x_odd)
        if n:
            part = project(basis, snaps, cx, cy, steps)
            a1, b1, part = lax.optimization_barrier((a1, b1, part))
            share = part if share is None else jnp.concatenate([share, part], axis=0)
        to_a, to_b = pack_for_y(state, a1, b1, cx, cy, nf)
        to_a, to_b, *rest = lax.optimization_barrier((to_a, to_b, *cuts[2:]))
        ya = lax.ppermute(to_a, BOTH, y_even)
        yb = lax.ppermute(to_b, BOTH, y_odd)
        a2 = lax.ppermute(rest[0], BOTH, x_even)
        b2 = lax.ppermute(rest[1], BOTH, x_odd)
        operands = (state, a1, b1, a2, b2, ya, yb, factors)
        state, snaps, *cuts = advance(operands, cx, cy, nf, steps, n == rounds - 1)
    sent = project(basis, snaps, cx, cy, steps, share, ns * nl)
    shares = lax.all_to_all(sent, BOTH, 0, 0)
    block, picks = pick_matrices(gram_old.shape[0], nl, sent)
    reduced, pod_gram, rhs_block = infer(shares, gram_old, picks, block)
    return (state.reshape(fields.shape), reduced, pod_gram, rhs_block)


def solution(mesh):
    in_specs = (P(None, "sim", "learn", None), P(), P(), P(None, None, "sim", "learn", None), P())
    out_specs = (P(None, "sim", "learn", None), P(), P(), P("learn", None))
    return jax.shard_map(body, mesh=mesh, in_specs=in_specs, out_specs=out_specs, check_vma=False)
```

```python
import functools

import jax
import jax.numpy as jnp
import numpy as np
from jax import lax
from jax.experimental import pallas as pl
from jax.experimental.pallas import tpu as pltpu
from jax.sharding import PartitionSpec as P


STEPS = 8

time_step = 0.1
drift_x = 1.2
drift_y = 1.0
drift_z = 0.3
arrhenius = 2.0
activation = 1.0

BOTH = ("sim", "learn")
VMEM = pl.BlockSpec(memory_space=pltpu.VMEM)
SMEM = pl.BlockSpec(memory_space=pltpu.SMEM)
MIB = 1024 * 1024


def both_ways(pairs):
    return [(a, b) for a, b in pairs] + [(b, a) for a, b in pairs]


def swaps(ns, nl):
    x_even = both_ways([(s * nl + l, (s + 1) * nl + l) for s in range(0, ns, 2) for l in range(nl)])
    x_odd = [(s * nl + l, (s + 1) * nl + l) for s in range(1, ns - 1, 2) for l in range(nl)]
    x_odd += [(s * nl + l, s * nl + l + 1) for s in (0, ns - 1) for l in range(0, nl, 2)]
    y_even = both_ways([(s * nl + l, s * nl + l + 1) for s in range(ns) for l in range(0, nl, 2)])
    y_odd = [(s * nl + l, s * nl + l + 1) for s in range(ns) for l in range(1, nl - 1, 2)]
    far = 2 if ns % 4 == 0 else 1
    y_far = y_odd + [(s * nl + l, (s + far) * nl + l) for s in range(ns) if s // far % 2 == 0 for l in (0, nl - 1)]
    y_odd = y_odd + [(s * nl, s * nl + nl - 1) for s in range(ns)]
    return x_even, both_ways(x_odd), y_even, both_ways(y_odd), both_ways(y_far)


def in_vmem(*arrays):
    return [pltpu.with_memory_space_constraint(a, pltpu.VMEM) for a in arrays]


def corner_runs(reach):
    runs, first = [], 0
    for d in range(1, reach):
        runs.append((d, reach - d, first))
        first += reach - d
    return runs, first


def x_runs(reach, cy):
    parts, sizes = ([], []), [0, 0]
    for d in range(1, reach + 1):
        count = min(reach - d, cy)
        if 2 * count >= cy:
            cuts = ((0, 0, cy),)
        else:
            cuts = ((0, 0, count), (1, count, cy - count), (0, cy - count, cy))
        for part, low, high in cuts:
            if high > low:
                parts[part].append((d, low, high - low, sizes[part]))
                sizes[part] += high - low
    return parts, sizes


def in_first_part(reach, cy, d, y):
    for e, low, count, first in x_runs(reach, cy)[0][0]:
        if e == d and low <= y < low + count:
            return first + y - low
    raise ValueError((d, y))


def each_case(cond, body):
    pl.when(cond)(lambda: body(True))
    pl.when(jnp.logical_not(cond))(lambda: body(False))


def cut_bricks(cx, cy, nf, load, a1_ref, b1_ref, a2_ref, b2_ref):
    parts, _ = x_runs(cx, cy)

    def cut(s_is_even):
        for part, a_ref, b_ref in ((0, a1_ref, b1_ref), (1, a2_ref, b2_ref)):
            for out_ref, is_east in ((a_ref, s_is_even), (b_ref, not s_is_even)):
                for d, y, count, first in parts[part]:
                    out_ref[pl.ds(first * nf, count * nf), :] = load(cx - d if is_east else d - 1, y, count)

    each_case(lax.rem(lax.axis_index("sim"), 2) == 0, cut)


def cut_shapes(cx, cy, nf, nz):
    sizes = x_runs(cx, cy)[1]
    return [pltpu.VMEM((size * nf, nz), jnp.float32) for size in (sizes[0], sizes[0], sizes[1], sizes[1])]


def columns_kernel(cx, cy, native_ref, out_ref, *cut_refs):
    nf = native_ref.shape[0] // (cx * cy)
    for c in range(cx * cy):
        out_ref[pl.ds(c * nf, nf), :] = native_ref[pl.ds(c, nf, stride=cx * cy), :]
    cut_bricks(cx, cy, nf, lambda x, y, n: out_ref[pl.ds((x * cy + y) * nf, n * nf), :], *cut_refs)


def to_columns(fields):
    nf, cx, cy, nz = fields.shape
    return pl.pallas_call(
        functools.partial(columns_kernel, cx, cy),
        out_shape=[pltpu.VMEM((cx * cy * nf, nz), jnp.float32), *cut_shapes(cx, cy, nf, nz)],
        in_specs=[VMEM],
        out_specs=[VMEM] * 5,
        compiler_params=pltpu.CompilerParams(vmem_limit_bytes=2 * MIB),
        name="to_columns",
    )(*in_vmem(fields.reshape(nf * cx * cy, nz)))


def factors_kernel(dif_ref, sto_ref, after_ref, out_ref):
    del after_ref
    _, nf, nz = out_ref.shape
    field = lax.broadcasted_iota(jnp.int32, (nf, nz), 0)
    for n, ref in enumerate((dif_ref, sto_ref)):
        value = jnp.zeros((nf, nz), jnp.float32)
        for f in range(nf):
            value = jnp.where(field == f, ref[f], value)
        out_ref[n] = value


def field_factors(diffusivity, stoich, nz, after):
    return pl.pallas_call(
        factors_kernel,
        out_shape=pltpu.VMEM((2, diffusivity.shape[0], nz), jnp.float32),
        in_specs=[SMEM, SMEM, pl.BlockSpec(memory_space=pl.ANY)],
        out_specs=VMEM,
        compiler_params=pltpu.CompilerParams(vmem_limit_bytes=MIB),
        name="field_factors",
    )(diffusivity, stoich, after)


def pack_kernel(cx, cy, nf, xa_ref, xb_ref, to_a_ref, to_b_ref):
    runs, size = corner_runs(cx)

    def copy(l_is_even):
        for out_ref, north in ((to_a_ref, l_is_even), (to_b_ref, not l_is_even)):
            for side, brick in enumerate((xa_ref, xb_ref)):
                for d, count, first in runs:
                    row = in_first_part(cx, cy, d, cy - count if north else 0)
                    rows = brick[pl.ds(row * nf, count * nf), :]
                    out_ref[pl.ds((side * size + first) * nf, count * nf), :] = rows

    each_case(lax.rem(lax.axis_index("learn"), 2) == 0, copy)


def pack_corners(xa, xb, cx, cy, nf):
    nz = xa.shape[1]
    size = 2 * corner_runs(cx)[1]
    shape = pltpu.VMEM((size * nf, nz), jnp.float32)
    return pl.pallas_call(
        functools.partial(pack_kernel, cx, cy, nf),
        out_shape=(shape, shape),
        in_specs=[VMEM] * 2,
        out_specs=(VMEM, VMEM),
        compiler_params=pltpu.CompilerParams(vmem_limit_bytes=MIB),
        name="pack_corners",
    )(*in_vmem(xa, xb))


def load_kernel(source_ref, out_ref, sem):
    copy = pltpu.make_async_copy(source_ref, out_ref, sem)
    copy.start()
    copy.wait()


def load_basis(basis):
    return pl.pallas_call(
        load_kernel,
        out_shape=pltpu.VMEM(basis.shape, basis.dtype),
        in_specs=[pl.BlockSpec(memory_space=pltpu.HBM)],
        out_specs=VMEM,
        scratch_shapes=[pltpu.SemaphoreType.DMA],
        compiler_params=pltpu.CompilerParams(vmem_limit_bytes=MIB),
        name="load_basis",
    )(pltpu.with_memory_space_constraint(basis, pltpu.HBM))


def round_kernel(
    cx, cy, nf, steps, last, own_ref, a1_ref, b1_ref, a2_ref, b2_ref, ya_ref, yb_ref, ca_ref, cb_ref, factors_ref,
    state_ref, snap_ref, *refs,
):
    cut_refs, (u_ref, m_ref, rate_ref) = refs[:-3], refs[-3:]
    nz = own_ref.shape[1]
    reach = 2 * steps
    wide_x, wide_y = cx + 2 * reach, cy + 2 * reach
    s, l = lax.axis_index("sim"), lax.axis_index("learn")
    ns, nl = lax.axis_size("sim"), lax.axis_size("learn")
    even_s, even_l = lax.rem(s, 2) == 0, lax.rem(l, 2) == 0
    has_west, has_east = s > 0, s < ns - 1
    has_south, has_north = l > 0, l < nl - 1

    def place(ref, x0, y0):
        for i in range(cx):
            rows = ref[pl.ds(i * cy * nf, cy * nf), :]
            u_ref[pl.ds(((x0 + i) * wide_y + y0) * nf, cy * nf), :] = rows

    def halo_x(is_east, d):
        return reach + cx + d - 1 if is_east else reach - d

    def clear(x0, x1, y0, y1):
        zeros = jnp.zeros(((y1 - y0) * nf, nz), jnp.float32)

        def trip(x, carry):
            for ref in (u_ref, m_ref):
                ref[pl.ds(pl.multiple_of((x * wide_y + y0) * nf, nf), (y1 - y0) * nf), :] = zeros
            return carry

        lax.fori_loop(x0, x1, trip, 0)

    place(own_ref, reach, reach)
    corners, size = corner_runs(reach)
    parts, _ = x_runs(reach, cy)

    def receive_x(s_is_even):
        for first_ref, rest_ref, is_east in ((a1_ref, a2_ref, s_is_even), (b1_ref, b2_ref, not s_is_even)):

            @pl.when(has_east if is_east else has_west)
            def _(first_ref=first_ref, rest_ref=rest_ref, is_east=is_east):
                for ref, runs in ((first_ref, parts[0]), (rest_ref, parts[1])):
                    for d, y, count, first in runs:
                        rows = ref[pl.ds(first * nf, count * nf), :]
                        u_ref[pl.ds((halo_x(is_east, d) * wide_y + reach + y) * nf, count * nf), :] = rows

    def receive_y(l_is_even):
        for ref, corner, north in ((ya_ref, ca_ref, l_is_even), (yb_ref, cb_ref, not l_is_even)):

            @pl.when(has_north if north else has_south)
            def _(ref=ref, corner=corner, north=north):
                place(ref, reach, reach + cy if north else 0)

                def receive_corners(s_is_even):
                    for side in range(2):
                        for d, count, first in corners:
                            x = halo_x(s_is_even == (side == 0), d)
                            y = reach + cy if north else reach - count
                            rows = corner[pl.ds((side * size + first) * nf, count * nf), :]
                            u_ref[pl.ds((x * wide_y + y) * nf, count * nf), :] = rows

                each_case(even_s, receive_corners)

    each_case(even_s, receive_x)
    each_case(even_l, receive_y)
    pl.when(jnp.logical_not(has_west))(lambda: clear(0, reach, 0, wide_y))
    pl.when(jnp.logical_not(has_east))(lambda: clear(reach + cx, wide_x, 0, wide_y))
    pl.when(jnp.logical_not(has_south))(lambda: clear(0, wide_x, 0, reach))
    pl.when(jnp.logical_not(has_north))(lambda: clear(0, wide_x, reach + cy, wide_y))

    lane = lax.broadcasted_iota(jnp.int32, (nf, nz), 1)
    diffusivity, stoich = factors_ref[0], factors_ref[1]

    def coefficients(dt):
        return (
            1.0 * (dt / time_step) - 6.0 * dt * diffusivity,
            dt * (diffusivity - 0.5 * drift_x),
            dt * (diffusivity + 0.5 * drift_x),
            dt * (diffusivity - 0.5 * drift_y),
            dt * (diffusivity + 0.5 * drift_y),
            jnp.where(lane < nz - 1, dt * (diffusivity - 0.5 * drift_z), 0.0),
            jnp.where(lane > 0, dt * (diffusivity + 0.5 * drift_z), 0.0),
            dt * arrhenius * stoich,
        )

    in_south = jnp.where(has_south, 1.0, 0.0)
    in_north = jnp.where(has_north, 1.0, 0.0)

    def rows_block(src, dst, old, coefs, rows):
        cc, ce, cw, cn, cs, cu, cl, ck = coefs

        def load(x, y):
            return src[pl.ds((x * wide_y + y) * nf, nf), :]

        for k, (x, beyond) in enumerate(rows):
            y_first, width = reach - beyond, cy + 2 * beyond
            for p in range(0, width, nf):
                base = (x * wide_y + y_first + p) * nf
                u0 = src[pl.ds(base, nf, stride=nf), :]
                u1 = src[pl.ds(base + 1, nf, stride=nf), :]
                u7 = src[pl.ds(base + 7, nf, stride=nf), :]
                rate = jnp.tanh(u0) * jnp.tanh(u1) * jnp.exp(-activation / (1.0 + u7 * u7))
                rate_ref[pl.ds(k * (wide_y + nf) + p, nf), :] = rate
        for k, (x, beyond) in enumerate(rows):
            y_first, width = reach - beyond, cy + 2 * beyond
            south, centre = load(x, y_first - 1), load(x, y_first)
            for j in range(width):
                y = y_first + j
                north = load(x, y + 1)
                value = cc * centre + cn * north + cs * south
                value += ce * load(x + 1, y) + cw * load(x - 1, y)
                value += cu * pltpu.roll(centre, nz - 1, 1) + cl * pltpu.roll(centre, 1, 1)
                value += ck * rate_ref[pl.ds(k * (wide_y + nf) + j, nf, stride=0), :]
                if old is not None:
                    value += 0.5 * old[pl.ds((x * wide_y + y) * nf, nf), :]
                if y < reach:
                    value *= in_south
                if y >= reach + cy:
                    value *= in_north
                dst[pl.ds((x * wide_y + y) * nf, nf), :] = value
                south, centre = centre, north

    def stage(src, dst, old, r, coefs):
        group = 4

        def trip(i, carry):
            x0 = reach + i * group
            rows_block(src, dst, old, coefs, [(x0 + k, r) for k in range(group)])
            return carry

        lax.fori_loop(0, cx // group, trip, 0)
        if r:

            @pl.when(has_west)
            def _():
                rows_block(src, dst, old, coefs, [(reach - d, r - d) for d in range(1, r + 1)])

            @pl.when(has_east)
            def _():
                rows_block(src, dst, old, coefs, [(reach + cx - 1 + d, r - d) for d in range(1, r + 1)])

    whole, half = coefficients(time_step), coefficients(0.5 * time_step)
    for t in range(steps):
        r = reach - 1 - 2 * t
        stage(u_ref, m_ref, None, r, whole)
        stage(m_ref, u_ref, u_ref, r - 1, half)
        for x in range(cx):
            for f in range(nf):
                value = u_ref[pl.ds(((reach + x) * wide_y + reach) * nf + f, cy, stride=nf), :]
                snap_ref[f * cx + x, pl.ds(t * cy, cy), :] = value
                if last and t == steps - 1:
                    state_ref[pl.ds((f * cx + x) * cy, cy), :] = value
    if not last:
        for i in range(cx):
            rows = u_ref[pl.ds(((reach + i) * wide_y + reach) * nf, cy * nf), :]
            state_ref[pl.ds(i * cy * nf, cy * nf), :] = rows

        def brick(x, y, count):
            return u_ref[pl.ds(((reach + x) * wide_y + reach + y) * nf, count * nf), :]

        cut_bricks(cx, cy, nf, brick, *cut_refs)


def advance(operands, cx, cy, nf, steps, last):
    nz = operands[0].shape[1]
    wide = (cx + 4 * steps) * (cy + 4 * steps)
    rows = max(cx, 2 * steps) * (cy + 4 * steps + nf)
    shape = (nf * cx * cy, nz)
    cuts = [] if last else cut_shapes(cx, cy, nf, nz)
    return pl.pallas_call(
        functools.partial(round_kernel, cx, cy, nf, steps, last),
        out_shape=[
            pltpu.VMEM(shape, jnp.float32),
            pltpu.VMEM((nf * cx, steps * cy, nz), jnp.float32),
            *cuts,
        ],
        in_specs=[VMEM] * 10,
        out_specs=[VMEM] * (2 + len(cuts)),
        scratch_shapes=[
            pltpu.VMEM((wide * nf, nz), jnp.float32),
            pltpu.VMEM((wide * nf, nz), jnp.float32),
            pltpu.VMEM((rows, nz), jnp.float32),
        ],
        compiler_params=pltpu.CompilerParams(vmem_limit_bytes=8 * MIB),
        name="advance",
    )(*in_vmem(*operands))


def split(value):
    high = value.astype(jnp.bfloat16)
    rest = value - high.astype(jnp.float32)
    middle = rest.astype(jnp.bfloat16)
    return high, middle, (rest - middle.astype(jnp.float32)).astype(jnp.bfloat16)


def project_kernel(cx, cy, steps, copies, basis_ref, snap_ref, *refs):
    earlier_ref, out_ref, acc_ref = refs if copies else (None, *refs)
    modes, nf, _, nz = basis_ref.shape
    pair = 2
    for g in range(nf // pair):
        total = None
        for p in range(cx // 2):
            left, right = [], []
            for f in range(g * pair, (g + 1) * pair):
                left.append(basis_ref[:, f, pl.ds(p * 2 * cy, 2 * cy), :].reshape(modes * 2 * cy, nz))
                rows = snap_ref[pl.ds(f * cx + 2 * p, 2)].reshape(2 * steps * cy, nz)
                right.append(rows.astype(jnp.bfloat16))
            term = lax.dot_general(
                jnp.concatenate(right, axis=1),
                jnp.concatenate(left, axis=1),
                (((1,), (1,)), ((), ())),
                preferred_element_type=jnp.float32,
            )
            total = term if total is None else total + term
        acc_ref[...] = total if g == 0 else acc_ref[...] + total

    lanes = 8 * 2 * cy
    blocks = modes * 2 * cy // lanes
    row = lax.broadcasted_iota(jnp.int32, (cy, lanes), 0)
    column = lax.broadcasted_iota(jnp.int32, (cy, lanes), 1)
    same_y = row == lax.rem(column, cy)
    first_x = lax.rem(column // cy, 2) == 0
    mode_of = lax.broadcasted_iota(jnp.int32, (lanes, modes), 0) // (2 * cy)
    mode = lax.broadcasted_iota(jnp.int32, (lanes, modes), 1)
    summed = None
    for k in range(blocks):
        kept = []
        for t in range(steps):
            west = acc_ref[pl.ds(t * cy, cy), pl.ds(k * lanes, lanes)]
            east = acc_ref[pl.ds((steps + t) * cy, cy), pl.ds(k * lanes, lanes)]
            kept.append(jnp.where(same_y, jnp.where(first_x, west, east), 0.0))
        gather = (mode - 8 * k == mode_of).astype(jnp.bfloat16)
        term = jnp.dot(
            jnp.concatenate(split(jnp.concatenate(kept, axis=0)), axis=0), gather, preferred_element_type=jnp.float32
        )
        summed = term if summed is None else summed + term
    count = steps * cy
    summed = summed[:count] + summed[count : 2 * count] + summed[2 * count :]
    result = jnp.sum(summed.reshape(steps, cy, modes), axis=1)
    if copies:
        both = jnp.concatenate([earlier_ref[...], result], axis=0)
        for n in range(copies):
            out_ref[n] = both
    else:
        out_ref[...] = result


def project(basis, snaps, cx, cy, steps, earlier=None, copies=0):
    modes = basis.shape[0]
    shape = (steps, modes)
    operands = in_vmem(snaps)
    if copies:
        shape = (copies, earlier.shape[0] + steps, modes)
        operands += in_vmem(earlier)
    return pl.pallas_call(
        functools.partial(project_kernel, cx, cy, steps, copies),
        out_shape=jax.ShapeDtypeStruct(shape, jnp.float32) if copies else pltpu.VMEM(shape, jnp.float32),
        in_specs=[VMEM] * (1 + len(operands)),
        out_specs=VMEM,
        scratch_shapes=[pltpu.VMEM((2 * steps * cy, modes * 2 * cy), jnp.float32)],
        compiler_params=pltpu.CompilerParams(vmem_limit_bytes=8 * MIB),
        name="project",
    )(basis, *operands)


def pair_tables(modes):
    upper_pairs = np.triu_indices(modes)
    first_table = np.concatenate([np.zeros(modes), upper_pairs[0] + 1]).astype(np.int32)
    second_table = np.concatenate([np.arange(modes) + 1, upper_pairs[1] + 1]).astype(np.int32)
    return (first_table, second_table)


def infer_kernel(shares_ref, gram_ref, picks_ref, reduced_ref, pod_ref, rhs_ref):
    steps, modes = reduced_ref.shape
    block = rhs_ref.shape[1]
    reduced = shares_ref[0]
    for n in range(1, shares_ref.shape[0]):
        reduced += shares_ref[n]
    reduced_ref[...] = reduced
    transposed = (((0,), (0,)), ((), ()))
    pod_ref[...] = gram_ref[...] + lax.dot_general(
        reduced, reduced, transposed, precision=lax.Precision.HIGHEST, preferred_element_type=jnp.float32
    )
    wide = picks_ref.shape[0]
    padded = jnp.concatenate([reduced, jnp.zeros((steps, wide - modes), jnp.float32)], axis=1)
    lane = lax.broadcasted_iota(jnp.int32, (steps, wide), 1)
    widened = jnp.where(lane == 0, 1.0, pltpu.roll(padded, 1, 1))
    picked = jnp.dot(jnp.concatenate(split(widened), axis=0), picks_ref[...], preferred_element_type=jnp.float32)
    picked = picked[:steps] + picked[steps : 2 * steps] + picked[2 * steps :]
    features = picked[:, :block] * picked[:, picks_ref.shape[1] // 2 :][:, :block]
    row = lax.broadcasted_iota(jnp.int32, (steps, modes), 0)
    changes = jnp.where(row < steps - 1, pltpu.roll(reduced, steps - 1, 0) - reduced, 0.0)
    ch, cm, cl = split(changes)
    fh, fm, fl = split(features)
    rhs_ref[...] = lax.dot_general(
        jnp.concatenate([ch, ch, cm, ch, cm, cl], axis=0),
        jnp.concatenate([fh, fm, fh, fl, fm, fh], axis=0),
        transposed,
        preferred_element_type=jnp.float32,
    )


def picks_kernel(tables_ref, after_ref, out_ref):
    del after_ref
    index = tables_ref[pl.ds(lax.axis_index("learn"), 1), :]
    place = lax.broadcasted_iota(jnp.int32, out_ref.shape, 0)
    out_ref[...] = jnp.where(place == index, 1.0, 0.0).astype(jnp.bfloat16)


def pick_matrices(modes, nl, after):
    tables = np.stack(pair_tables(modes))
    block = tables.shape[1] // nl
    lanes = -(-block // 128) * 128
    tables = tables.reshape(2, nl, block).transpose(1, 0, 2)
    tables = np.pad(tables, ((0, 0), (0, 0), (0, lanes - block)), constant_values=-1).reshape(nl, 2 * lanes)
    wide = -(-(modes + 1) // 128) * 128
    return block, pl.pallas_call(
        picks_kernel,
        out_shape=pltpu.VMEM((wide, 2 * lanes), jnp.bfloat16),
        in_specs=[VMEM, pl.BlockSpec(memory_space=pl.ANY)],
        out_specs=VMEM,
        compiler_params=pltpu.CompilerParams(vmem_limit_bytes=4 * MIB),
        name="pick_matrices",
    )(jnp.asarray(tables), after)


def infer(shares, gram_old, picks, block):
    _, steps, modes = shares.shape
    reduced, pod_gram, rhs = pl.pallas_call(
        infer_kernel,
        out_shape=(
            jax.ShapeDtypeStruct((steps, modes), jnp.float32),
            jax.ShapeDtypeStruct((modes, modes), jnp.float32),
            jax.ShapeDtypeStruct((modes, block), jnp.float32),
        ),
        in_specs=[VMEM] * 3,
        out_specs=(VMEM, VMEM, VMEM),
        compiler_params=pltpu.CompilerParams(vmem_limit_bytes=8 * MIB),
        name="infer",
    )(*in_vmem(shares, gram_old, picks))
    return reduced.T, pod_gram, rhs.T


def swap(value, pairs):
    return lax.ppermute(value, BOTH, pairs)


def body(fields, diffusivity, stoich, basis, gram_old):
    nf, cx, cy, nz = fields.shape
    ns, nl = lax.axis_size("sim"), lax.axis_size("learn")
    steps = min(cx, cy) // 2
    rounds = STEPS // steps
    x_even, x_odd, y_even, y_odd, y_far = swaps(ns, nl)
    state, *cuts = to_columns(fields)
    factors = field_factors(diffusivity, stoich, nz, state)
    share = None
    for n in range(rounds):
        a1, b1 = swap(cuts[0], x_even), swap(cuts[1], x_odd)
        ya, yb = swap(state, y_even), swap(state, y_odd)
        a2, b2 = swap(cuts[2], x_even), swap(cuts[3], x_odd)
        if n == 0:
            basis = load_basis(basis.reshape(basis.shape[0], nf, cx * cy, nz))
            a1, b1, basis, factors = lax.optimization_barrier((a1, b1, basis, factors))
        else:
            part = project(basis, snaps, cx, cy, steps)
            a1, b1, part = lax.optimization_barrier((a1, b1, part))
            share = part if share is None else jnp.concatenate([share, part], axis=0)
        to_a, to_b = pack_corners(a1, b1, cx, cy, nf)
        ca, cb = swap(to_a, y_even), swap(to_b, y_far)
        operands = (state, a1, b1, a2, b2, ya, yb, ca, cb, factors)
        state, snaps, *cuts = advance(operands, cx, cy, nf, steps, n == rounds - 1)
    sent = project(basis, snaps, cx, cy, steps, share, ns * nl)
    shares = lax.all_to_all(sent, BOTH, 0, 0)
    block, picks = pick_matrices(gram_old.shape[0], nl, sent)
    reduced, pod_gram, rhs_block = infer(shares, gram_old, picks, block)
    return (state.reshape(fields.shape), reduced, pod_gram, rhs_block)


def solution(mesh):
    in_specs = (P(None, "sim", "learn", None), P(), P(), P(None, None, "sim", "learn", None), P())
    out_specs = (P(None, "sim", "learn", None), P(), P(), P("learn", None))
    return jax.shard_map(body, mesh=mesh, in_specs=in_specs, out_specs=out_specs, check_vma=False)
```

```python
import functools

import jax
import jax.numpy as jnp
import numpy as np
from jax import lax
from jax.experimental import pallas as pl
from jax.experimental.pallas import tpu as pltpu
from jax.sharding import PartitionSpec as P


STEPS = 8

time_step = 0.1
drift_x = 1.2
drift_y = 1.0
drift_z = 0.3
arrhenius = 2.0
activation = 1.0

BOTH = ("sim", "learn")
VMEM = pl.BlockSpec(memory_space=pltpu.VMEM)
SMEM = pl.BlockSpec(memory_space=pltpu.SMEM)
MIB = 1024 * 1024


def both_ways(pairs):
    return [(a, b) for a, b in pairs] + [(b, a) for a, b in pairs]


def swaps(ns, nl):
    x_even = both_ways([(s * nl + l, (s + 1) * nl + l) for s in range(0, ns, 2) for l in range(nl)])
    x_odd = [(s * nl + l, (s + 1) * nl + l) for s in range(1, ns - 1, 2) for l in range(nl)]
    x_odd += [(s * nl + l, s * nl + l + 1) for s in (0, ns - 1) for l in range(0, nl, 2)]
    y_even = both_ways([(s * nl + l, s * nl + l + 1) for s in range(ns) for l in range(0, nl, 2)])
    y_odd = [(s * nl + l, s * nl + l + 1) for s in range(ns) for l in range(1, nl - 1, 2)]
    far = 2 if ns % 4 == 0 else 1
    y_far = y_odd + [(s * nl + l, (s + far) * nl + l) for s in range(ns) if s // far % 2 == 0 for l in (0, nl - 1)]
    y_odd = y_odd + [(s * nl, s * nl + nl - 1) for s in range(ns)]
    return x_even, both_ways(x_odd), y_even, both_ways(y_odd), both_ways(y_far)


def in_vmem(*arrays):
    return [pltpu.with_memory_space_constraint(a, pltpu.VMEM) for a in arrays]


def corner_runs(reach):
    runs, first = [], 0
    for d in range(1, reach):
        runs.append((d, reach - d, first))
        first += reach - d
    return runs, first


def x_runs(reach, cy):
    parts, sizes = ([], []), [0, 0]
    for d in range(1, reach + 1):
        count = min(reach - d, cy)
        if 2 * count >= cy:
            cuts = ((0, 0, cy),)
        else:
            cuts = ((0, 0, count), (1, count, cy - count), (0, cy - count, cy))
        for part, low, high in cuts:
            if high > low:
                parts[part].append((d, low, high - low, sizes[part]))
                sizes[part] += high - low
    return parts, sizes


def in_first_part(reach, cy, d, y):
    for e, low, count, first in x_runs(reach, cy)[0][0]:
        if e == d and low <= y < low + count:
            return first + y - low
    raise ValueError((d, y))


def each_case(cond, body):
    pl.when(cond)(lambda: body(True))
    pl.when(jnp.logical_not(cond))(lambda: body(False))


def cut_bricks(cx, cy, nf, load, a1_ref, b1_ref, a2_ref, b2_ref):
    parts, _ = x_runs(cx, cy)

    def cut(s_is_even):
        for part, a_ref, b_ref in ((0, a1_ref, b1_ref), (1, a2_ref, b2_ref)):
            for out_ref, is_east in ((a_ref, s_is_even), (b_ref, not s_is_even)):
                for d, y, count, first in parts[part]:
                    out_ref[pl.ds(first * nf, count * nf), :] = load(cx - d if is_east else d - 1, y, count)

    each_case(lax.rem(lax.axis_index("sim"), 2) == 0, cut)


def cut_shapes(cx, cy, nf, nz):
    sizes = x_runs(cx, cy)[1]
    return [pltpu.VMEM((size * nf, nz), jnp.float32) for size in (sizes[0], sizes[0], sizes[1], sizes[1])]


def columns_kernel(cx, cy, native_ref, out_ref, *cut_refs):
    nf = native_ref.shape[0] // (cx * cy)
    for c in range(cx * cy):
        out_ref[pl.ds(c * nf, nf), :] = native_ref[pl.ds(c, nf, stride=cx * cy), :]
    cut_bricks(cx, cy, nf, lambda x, y, n: out_ref[pl.ds((x * cy + y) * nf, n * nf), :], *cut_refs)


def to_columns(fields):
    nf, cx, cy, nz = fields.shape
    return pl.pallas_call(
        functools.partial(columns_kernel, cx, cy),
        out_shape=[pltpu.VMEM((cx * cy * nf, nz), jnp.float32), *cut_shapes(cx, cy, nf, nz)],
        in_specs=[VMEM],
        out_specs=[VMEM] * 5,
        compiler_params=pltpu.CompilerParams(vmem_limit_bytes=2 * MIB),
        name="to_columns",
    )(*in_vmem(fields.reshape(nf * cx * cy, nz)))


def factors_kernel(dif_ref, sto_ref, after_ref, out_ref):
    del after_ref
    _, nf, nz = out_ref.shape
    field = lax.broadcasted_iota(jnp.int32, (nf, nz), 0)
    for n, ref in enumerate((dif_ref, sto_ref)):
        value = jnp.zeros((nf, nz), jnp.float32)
        for f in range(nf):
            value = jnp.where(field == f, ref[f], value)
        out_ref[n] = value


def field_factors(diffusivity, stoich, nz, after):
    return pl.pallas_call(
        factors_kernel,
        out_shape=pltpu.VMEM((2, diffusivity.shape[0], nz), jnp.float32),
        in_specs=[SMEM, SMEM, pl.BlockSpec(memory_space=pl.ANY)],
        out_specs=VMEM,
        compiler_params=pltpu.CompilerParams(vmem_limit_bytes=MIB),
        name="field_factors",
    )(diffusivity, stoich, after)


def pack_kernel(cx, cy, nf, xa_ref, xb_ref, after_ref, to_a_ref, to_b_ref):
    del after_ref
    runs, size = corner_runs(cx)

    def copy(l_is_even):
        for out_ref, north in ((to_a_ref, l_is_even), (to_b_ref, not l_is_even)):
            for side, brick in enumerate((xa_ref, xb_ref)):
                for d, count, first in runs:
                    row = in_first_part(cx, cy, d, cy - count if north else 0)
                    rows = brick[pl.ds(row * nf, count * nf), :]
                    out_ref[pl.ds((side * size + first) * nf, count * nf), :] = rows

    each_case(lax.rem(lax.axis_index("learn"), 2) == 0, copy)


def pack_corners(xa, xb, after, cx, cy, nf):
    nz = xa.shape[1]
    size = 2 * corner_runs(cx)[1]
    shape = pltpu.VMEM((size * nf, nz), jnp.float32)
    return pl.pallas_call(
        functools.partial(pack_kernel, cx, cy, nf),
        out_shape=(shape, shape),
        in_specs=[VMEM, VMEM, pl.BlockSpec(memory_space=pl.ANY)],
        out_specs=(VMEM, VMEM),
        compiler_params=pltpu.CompilerParams(vmem_limit_bytes=MIB),
        name="pack_corners",
    )(*in_vmem(xa, xb), after)


def load_kernel(source_ref, out_ref, sem):
    copy = pltpu.make_async_copy(source_ref, out_ref, sem)
    copy.start()
    copy.wait()


def load_basis(basis):
    return pl.pallas_call(
        load_kernel,
        out_shape=pltpu.VMEM(basis.shape, basis.dtype),
        in_specs=[pl.BlockSpec(memory_space=pltpu.HBM)],
        out_specs=VMEM,
        scratch_shapes=[pltpu.SemaphoreType.DMA],
        compiler_params=pltpu.CompilerParams(vmem_limit_bytes=MIB),
        name="load_basis",
    )(pltpu.with_memory_space_constraint(basis, pltpu.HBM))


def round_kernel(
    cx, cy, nf, steps, last, own_ref, a1_ref, b1_ref, a2_ref, b2_ref, ya_ref, yb_ref, ca_ref, cb_ref, factors_ref,
    state_ref, snap_ref, *refs,
):
    cut_refs, (u_ref, m_ref, rate_ref) = refs[:-3], refs[-3:]
    nz = own_ref.shape[1]
    reach = 2 * steps
    wide_x, wide_y = cx + 2 * reach, cy + 2 * reach
    s, l = lax.axis_index("sim"), lax.axis_index("learn")
    ns, nl = lax.axis_size("sim"), lax.axis_size("learn")
    even_s, even_l = lax.rem(s, 2) == 0, lax.rem(l, 2) == 0
    has_west, has_east = s > 0, s < ns - 1
    has_south, has_north = l > 0, l < nl - 1

    def place(ref, x0, y0):
        for i in range(cx):
            rows = ref[pl.ds(i * cy * nf, cy * nf), :]
            u_ref[pl.ds(((x0 + i) * wide_y + y0) * nf, cy * nf), :] = rows

    def halo_x(is_east, d):
        return reach + cx + d - 1 if is_east else reach - d

    def clear(x0, x1, y0, y1):
        zeros = jnp.zeros(((y1 - y0) * nf, nz), jnp.float32)

        def trip(x, carry):
            for ref in (u_ref, m_ref):
                ref[pl.ds(pl.multiple_of((x * wide_y + y0) * nf, nf), (y1 - y0) * nf), :] = zeros
            return carry

        lax.fori_loop(x0, x1, trip, 0)

    place(own_ref, reach, reach)
    corners, size = corner_runs(reach)
    parts, _ = x_runs(reach, cy)

    def receive_x(s_is_even):
        for first_ref, rest_ref, is_east in ((a1_ref, a2_ref, s_is_even), (b1_ref, b2_ref, not s_is_even)):

            @pl.when(has_east if is_east else has_west)
            def _(first_ref=first_ref, rest_ref=rest_ref, is_east=is_east):
                for ref, runs in ((first_ref, parts[0]), (rest_ref, parts[1])):
                    for d, y, count, first in runs:
                        rows = ref[pl.ds(first * nf, count * nf), :]
                        u_ref[pl.ds((halo_x(is_east, d) * wide_y + reach + y) * nf, count * nf), :] = rows

    def receive_y(l_is_even):
        for ref, corner, north in ((ya_ref, ca_ref, l_is_even), (yb_ref, cb_ref, not l_is_even)):

            @pl.when(has_north if north else has_south)
            def _(ref=ref, corner=corner, north=north):
                place(ref, reach, reach + cy if north else 0)

                def receive_corners(s_is_even):
                    for side in range(2):
                        for d, count, first in corners:
                            x = halo_x(s_is_even == (side == 0), d)
                            y = reach + cy if north else reach - count
                            rows = corner[pl.ds((side * size + first) * nf, count * nf), :]
                            u_ref[pl.ds((x * wide_y + y) * nf, count * nf), :] = rows

                each_case(even_s, receive_corners)

    each_case(even_s, receive_x)
    each_case(even_l, receive_y)
    pl.when(jnp.logical_not(has_west))(lambda: clear(0, reach, 0, wide_y))
    pl.when(jnp.logical_not(has_east))(lambda: clear(reach + cx, wide_x, 0, wide_y))
    pl.when(jnp.logical_not(has_south))(lambda: clear(0, wide_x, 0, reach))
    pl.when(jnp.logical_not(has_north))(lambda: clear(0, wide_x, reach + cy, wide_y))

    lane = lax.broadcasted_iota(jnp.int32, (nf, nz), 1)
    diffusivity, stoich = factors_ref[0], factors_ref[1]

    def coefficients(dt):
        return (
            1.0 * (dt / time_step) - 6.0 * dt * diffusivity,
            dt * (diffusivity - 0.5 * drift_x),
            dt * (diffusivity + 0.5 * drift_x),
            dt * (diffusivity - 0.5 * drift_y),
            dt * (diffusivity + 0.5 * drift_y),
            jnp.where(lane < nz - 1, dt * (diffusivity - 0.5 * drift_z), 0.0),
            jnp.where(lane > 0, dt * (diffusivity + 0.5 * drift_z), 0.0),
            dt * arrhenius * stoich,
        )

    in_south = jnp.where(has_south, 1.0, 0.0)
    in_north = jnp.where(has_north, 1.0, 0.0)

    def rows_block(src, dst, old, coefs, rows):
        cc, ce, cw, cn, cs, cu, cl, ck = coefs

        def load(x, y):
            return src[pl.ds((x * wide_y + y) * nf, nf), :]

        for k, (x, beyond) in enumerate(rows):
            y_first, width = reach - beyond, cy + 2 * beyond
            for p in range(0, width, nf):
                base = (x * wide_y + y_first + p) * nf
                u0 = src[pl.ds(base, nf, stride=nf), :]
                u1 = src[pl.ds(base + 1, nf, stride=nf), :]
                u7 = src[pl.ds(base + 7, nf, stride=nf), :]
                rate = jnp.tanh(u0) * jnp.tanh(u1) * jnp.exp(-activation / (1.0 + u7 * u7))
                rate_ref[pl.ds(k * (wide_y + nf) + p, nf), :] = rate
        for k, (x, beyond) in enumerate(rows):
            y_first, width = reach - beyond, cy + 2 * beyond
            south, centre = load(x, y_first - 1), load(x, y_first)
            for j in range(width):
                y = y_first + j
                north = load(x, y + 1)
                value = cc * centre + cn * north + cs * south
                value += ce * load(x + 1, y) + cw * load(x - 1, y)
                value += cu * pltpu.roll(centre, nz - 1, 1) + cl * pltpu.roll(centre, 1, 1)
                value += ck * rate_ref[pl.ds(k * (wide_y + nf) + j, nf, stride=0), :]
                if old is not None:
                    value += 0.5 * old[pl.ds((x * wide_y + y) * nf, nf), :]
                if y < reach:
                    value *= in_south
                if y >= reach + cy:
                    value *= in_north
                dst[pl.ds((x * wide_y + y) * nf, nf), :] = value
                south, centre = centre, north

    def stage(src, dst, old, r, coefs):
        group = 4

        def trip(i, carry):
            x0 = reach + i * group
            rows_block(src, dst, old, coefs, [(x0 + k, r) for k in range(group)])
            return carry

        lax.fori_loop(0, cx // group, trip, 0)
        if r:

            @pl.when(has_west)
            def _():
                rows_block(src, dst, old, coefs, [(reach - d, r - d) for d in range(1, r + 1)])

            @pl.when(has_east)
            def _():
                rows_block(src, dst, old, coefs, [(reach + cx - 1 + d, r - d) for d in range(1, r + 1)])

    whole, half = coefficients(time_step), coefficients(0.5 * time_step)
    for t in range(steps):
        r = reach - 1 - 2 * t
        stage(u_ref, m_ref, None, r, whole)
        stage(m_ref, u_ref, u_ref, r - 1, half)
        for x in range(cx):
            for f in range(nf):
                value = u_ref[pl.ds(((reach + x) * wide_y + reach) * nf + f, cy, stride=nf), :]
                snap_ref[f * cx + x, pl.ds(t * cy, cy), :] = value
                if last and t == steps - 1:
                    state_ref[pl.ds((f * cx + x) * cy, cy), :] = value
    if not last:
        for i in range(cx):
            rows = u_ref[pl.ds(((reach + i) * wide_y + reach) * nf, cy * nf), :]
            state_ref[pl.ds(i * cy * nf, cy * nf), :] = rows

        def brick(x, y, count):
            return u_ref[pl.ds(((reach + x) * wide_y + reach + y) * nf, count * nf), :]

        cut_bricks(cx, cy, nf, brick, *cut_refs)


def advance(operands, cx, cy, nf, steps, last):
    nz = operands[0].shape[1]
    wide = (cx + 4 * steps) * (cy + 4 * steps)
    rows = max(cx, 2 * steps) * (cy + 4 * steps + nf)
    shape = (nf * cx * cy, nz)
    cuts = [] if last else cut_shapes(cx, cy, nf, nz)
    return pl.pallas_call(
        functools.partial(round_kernel, cx, cy, nf, steps, last),
        out_shape=[
            pltpu.VMEM(shape, jnp.float32),
            pltpu.VMEM((nf * cx, steps * cy, nz), jnp.float32),
            *cuts,
        ],
        in_specs=[VMEM] * 10,
        out_specs=[VMEM] * (2 + len(cuts)),
        scratch_shapes=[
            pltpu.VMEM((wide * nf, nz), jnp.float32),
            pltpu.VMEM((wide * nf, nz), jnp.float32),
            pltpu.VMEM((rows, nz), jnp.float32),
        ],
        compiler_params=pltpu.CompilerParams(vmem_limit_bytes=8 * MIB),
        name="advance",
    )(*in_vmem(*operands))


def split(value):
    high = value.astype(jnp.bfloat16)
    rest = value - high.astype(jnp.float32)
    middle = rest.astype(jnp.bfloat16)
    return high, middle, (rest - middle.astype(jnp.float32)).astype(jnp.bfloat16)


def project_kernel(cx, cy, steps, first, end, copies, basis_ref, snap_ref, *refs):
    earlier_ref, out_ref, acc_ref = refs if len(refs) == 3 else (None, *refs)
    modes, _, _, nz = basis_ref.shape
    pair = 2
    for g in range(first // pair, end // pair):
        total = None
        for p in range(cx // 2):
            left, right = [], []
            for f in range(g * pair, (g + 1) * pair):
                left.append(basis_ref[:, f, pl.ds(p * 2 * cy, 2 * cy), :].reshape(modes * 2 * cy, nz))
                rows = snap_ref[pl.ds(f * cx + 2 * p, 2)].reshape(2 * steps * cy, nz)
                right.append(rows.astype(jnp.bfloat16))
            term = lax.dot_general(
                jnp.concatenate(right, axis=1),
                jnp.concatenate(left, axis=1),
                (((1,), (1,)), ((), ())),
                preferred_element_type=jnp.float32,
            )
            total = term if total is None else total + term
        acc_ref[...] = total if g == first // pair else acc_ref[...] + total

    lanes = 8 * 2 * cy
    blocks = modes * 2 * cy // lanes
    row = lax.broadcasted_iota(jnp.int32, (cy, lanes), 0)
    column = lax.broadcasted_iota(jnp.int32, (cy, lanes), 1)
    same_y = row == lax.rem(column, cy)
    first_x = lax.rem(column // cy, 2) == 0
    mode_of = lax.broadcasted_iota(jnp.int32, (lanes, modes), 0) // (2 * cy)
    mode = lax.broadcasted_iota(jnp.int32, (lanes, modes), 1)
    summed = None
    for k in range(blocks):
        kept = []
        for t in range(steps):
            west = acc_ref[pl.ds(t * cy, cy), pl.ds(k * lanes, lanes)]
            east = acc_ref[pl.ds((steps + t) * cy, cy), pl.ds(k * lanes, lanes)]
            kept.append(jnp.where(same_y, jnp.where(first_x, west, east), 0.0))
        gather = (mode - 8 * k == mode_of).astype(jnp.bfloat16)
        term = jnp.dot(
            jnp.concatenate(split(jnp.concatenate(kept, axis=0)), axis=0), gather, preferred_element_type=jnp.float32
        )
        summed = term if summed is None else summed + term
    count = steps * cy
    summed = summed[:count] + summed[count : 2 * count] + summed[2 * count :]
    result = jnp.sum(summed.reshape(steps, cy, modes), axis=1)
    if copies:
        both = jnp.concatenate([earlier_ref[...], result], axis=0)
        for n in range(copies):
            out_ref[n] = both
    else:
        out_ref[...] = result if earlier_ref is None else earlier_ref[...] + result


def project(basis, snaps, cx, cy, steps, fields, earlier=None, copies=0):
    modes = basis.shape[0]
    shape = (steps, modes)
    operands = in_vmem(snaps)
    if copies:
        shape = (copies, earlier.shape[0] + steps, modes)
    if earlier is not None:
        operands += in_vmem(earlier)
    return pl.pallas_call(
        functools.partial(project_kernel, cx, cy, steps, *fields, copies),
        out_shape=jax.ShapeDtypeStruct(shape, jnp.float32) if copies else pltpu.VMEM(shape, jnp.float32),
        in_specs=[VMEM] * (1 + len(operands)),
        out_specs=VMEM,
        scratch_shapes=[pltpu.VMEM((2 * steps * cy, modes * 2 * cy), jnp.float32)],
        compiler_params=pltpu.CompilerParams(vmem_limit_bytes=8 * MIB),
    )(basis, *operands)


def pair_tables(modes):
    upper_pairs = np.triu_indices(modes)
    first_table = np.concatenate([np.zeros(modes), upper_pairs[0] + 1]).astype(np.int32)
    second_table = np.concatenate([np.arange(modes) + 1, upper_pairs[1] + 1]).astype(np.int32)
    return (first_table, second_table)


def infer_kernel(shares_ref, gram_ref, picks_ref, reduced_ref, pod_ref, rhs_ref):
    steps, modes = reduced_ref.shape
    block = rhs_ref.shape[1]
    reduced = shares_ref[0]
    for n in range(1, shares_ref.shape[0]):
        reduced += shares_ref[n]
    reduced_ref[...] = reduced
    transposed = (((0,), (0,)), ((), ()))
    pod_ref[...] = gram_ref[...] + lax.dot_general(
        reduced, reduced, transposed, precision=lax.Precision.HIGHEST, preferred_element_type=jnp.float32
    )
    wide = picks_ref.shape[0]
    padded = jnp.concatenate([reduced, jnp.zeros((steps, wide - modes), jnp.float32)], axis=1)
    lane = lax.broadcasted_iota(jnp.int32, (steps, wide), 1)
    widened = jnp.where(lane == 0, 1.0, pltpu.roll(padded, 1, 1))
    picked = jnp.dot(jnp.concatenate(split(widened), axis=0), picks_ref[...], preferred_element_type=jnp.float32)
    picked = picked[:steps] + picked[steps : 2 * steps] + picked[2 * steps :]
    features = picked[:, :block] * picked[:, picks_ref.shape[1] // 2 :][:, :block]
    row = lax.broadcasted_iota(jnp.int32, (steps, modes), 0)
    changes = jnp.where(row < steps - 1, pltpu.roll(reduced, steps - 1, 0) - reduced, 0.0)
    ch, cm, cl = split(changes)
    fh, fm, fl = split(features)
    rhs_ref[...] = lax.dot_general(
        jnp.concatenate([ch, ch, cm, ch, cm, cl], axis=0),
        jnp.concatenate([fh, fm, fh, fl, fm, fh], axis=0),
        transposed,
        preferred_element_type=jnp.float32,
    )


def picks_kernel(tables_ref, after_ref, out_ref):
    del after_ref
    index = tables_ref[pl.ds(lax.axis_index("learn"), 1), :]
    place = lax.broadcasted_iota(jnp.int32, out_ref.shape, 0)
    out_ref[...] = jnp.where(place == index, 1.0, 0.0).astype(jnp.bfloat16)


def pick_matrices(modes, nl, after):
    tables = np.stack(pair_tables(modes))
    block = tables.shape[1] // nl
    lanes = -(-block // 128) * 128
    tables = tables.reshape(2, nl, block).transpose(1, 0, 2)
    tables = np.pad(tables, ((0, 0), (0, 0), (0, lanes - block)), constant_values=-1).reshape(nl, 2 * lanes)
    wide = -(-(modes + 1) // 128) * 128
    return block, pl.pallas_call(
        picks_kernel,
        out_shape=pltpu.VMEM((wide, 2 * lanes), jnp.bfloat16),
        in_specs=[VMEM, pl.BlockSpec(memory_space=pl.ANY)],
        out_specs=VMEM,
        compiler_params=pltpu.CompilerParams(vmem_limit_bytes=4 * MIB),
        name="pick_matrices",
    )(jnp.asarray(tables), after)


def infer(shares, gram_old, picks, block):
    _, steps, modes = shares.shape
    reduced, pod_gram, rhs = pl.pallas_call(
        infer_kernel,
        out_shape=(
            jax.ShapeDtypeStruct((steps, modes), jnp.float32),
            jax.ShapeDtypeStruct((modes, modes), jnp.float32),
            jax.ShapeDtypeStruct((modes, block), jnp.float32),
        ),
        in_specs=[VMEM] * 3,
        out_specs=(VMEM, VMEM, VMEM),
        compiler_params=pltpu.CompilerParams(vmem_limit_bytes=8 * MIB),
        name="infer",
    )(*in_vmem(shares, gram_old, picks))
    return reduced.T, pod_gram, rhs.T


def swap(value, pairs):
    return lax.ppermute(value, BOTH, pairs)


def mark_kernel(after_ref, out_ref):
    del after_ref
    out_ref[...] = jnp.zeros_like(out_ref)


def mark(after):
    return pl.pallas_call(
        mark_kernel,
        out_shape=pltpu.VMEM((8, after.shape[1]), after.dtype),
        in_specs=[pl.BlockSpec(memory_space=pl.ANY)],
        out_specs=VMEM,
        compiler_params=pltpu.CompilerParams(vmem_limit_bytes=MIB),
        name="mark",
    )(after)


def body(fields, diffusivity, stoich, basis, gram_old):
    nf, cx, cy, nz = fields.shape
    ns, nl = lax.axis_size("sim"), lax.axis_size("learn")
    steps = min(cx, cy) // 2
    rounds = STEPS // steps
    x_even, x_odd, y_even, y_odd, y_far = swaps(ns, nl)
    state, *cuts = to_columns(fields)
    share = None
    for n in range(rounds):
        a1, b1 = swap(cuts[0], x_even), swap(cuts[1], x_odd)
        ya, yb = swap(state, y_even), swap(state, y_odd)
        a2, b2 = swap(cuts[2], x_even), swap(cuts[3], x_odd)
        if n == 0:
            basis = load_basis(basis.reshape(basis.shape[0], nf, cx * cy, nz))
        else:
            part = project(basis, snaps, cx, cy, steps, (0, nf // 2))
        to_a, to_b = pack_corners(a1, b1, mark(state), cx, cy, nf)
        ca, cb = swap(to_a, y_even), swap(to_b, y_far)
        if n == 0:
            factors = field_factors(diffusivity, stoich, nz, to_b)
        else:
            part = project(basis, snaps, cx, cy, steps, (nf // 2, nf), part)
            share = part if share is None else jnp.concatenate([share, part], axis=0)
        operands = (state, a1, b1, a2, b2, ya, yb, ca, cb, factors)
        state, snaps, *cuts = advance(operands, cx, cy, nf, steps, n == rounds - 1)
    sent = project(basis, snaps, cx, cy, steps, (0, nf), share, ns * nl)
    shares = lax.all_to_all(sent, BOTH, 0, 0)
    block, picks = pick_matrices(gram_old.shape[0], nl, sent)
    reduced, pod_gram, rhs_block = infer(shares, gram_old, picks, block)
    return (state.reshape(fields.shape), reduced, pod_gram, rhs_block)


def solution(mesh):
    in_specs = (P(None, "sim", "learn", None), P(), P(), P(None, None, "sim", "learn", None), P())
    out_specs = (P(None, "sim", "learn", None), P(), P(), P("learn", None))
    return jax.shard_map(body, mesh=mesh, in_specs=in_specs, out_specs=out_specs, check_vma=False)
```

```python
import functools

import jax
import jax.numpy as jnp
import numpy as np
from jax import lax
from jax.experimental import pallas as pl
from jax.experimental.pallas import tpu as pltpu
from jax.sharding import PartitionSpec as P


STEPS = 8

time_step = 0.1
drift_x = 1.2
drift_y = 1.0
drift_z = 0.3
arrhenius = 2.0
activation = 1.0

BOTH = ("sim", "learn")
VMEM = pl.BlockSpec(memory_space=pltpu.VMEM)
SMEM = pl.BlockSpec(memory_space=pltpu.SMEM)
MIB = 1024 * 1024


def both_ways(pairs):
    return [(a, b) for a, b in pairs] + [(b, a) for a, b in pairs]


def swaps(ns, nl):
    x_even = both_ways([(s * nl + l, (s + 1) * nl + l) for s in range(0, ns, 2) for l in range(nl)])
    x_odd = [(s * nl + l, (s + 1) * nl + l) for s in range(1, ns - 1, 2) for l in range(nl)]
    x_odd += [(s * nl + l, s * nl + l + 1) for s in (0, ns - 1) for l in range(0, nl, 2)]
    y_even = both_ways([(s * nl + l, s * nl + l + 1) for s in range(ns) for l in range(0, nl, 2)])
    y_odd = [(s * nl + l, s * nl + l + 1) for s in range(ns) for l in range(1, nl - 1, 2)]
    far = 2 if ns % 4 == 0 else 1
    y_far = y_odd + [(s * nl + l, (s + far) * nl + l) for s in range(ns) if s // far % 2 == 0 for l in (0, nl - 1)]
    y_odd = y_odd + [(s * nl, s * nl + nl - 1) for s in range(ns)]
    return x_even, both_ways(x_odd), y_even, both_ways(y_odd), both_ways(y_far)


def in_vmem(*arrays):
    return [pltpu.with_memory_space_constraint(a, pltpu.VMEM) for a in arrays]


def corner_runs(reach):
    runs, first = [], 0
    for d in range(1, reach):
        runs.append((d, reach - d, first))
        first += reach - d
    return runs, first


def x_runs(reach, cy):
    parts, sizes = ([], []), [0, 0]
    for d in range(1, reach + 1):
        count = min(reach - d, cy)
        if 2 * count >= cy:
            cuts = ((0, 0, cy),)
        else:
            cuts = ((0, 0, count), (1, count, cy - count), (0, cy - count, cy))
        for part, low, high in cuts:
            if high > low:
                parts[part].append((d, low, high - low, sizes[part]))
                sizes[part] += high - low
    return parts, sizes


def in_first_part(reach, cy, d, y):
    for e, low, count, first in x_runs(reach, cy)[0][0]:
        if e == d and low <= y < low + count:
            return first + y - low
    raise ValueError((d, y))


def each_case(cond, body):
    pl.when(cond)(lambda: body(True))
    pl.when(jnp.logical_not(cond))(lambda: body(False))


def cut_bricks(cx, cy, nf, load, a1_ref, b1_ref, a2_ref, b2_ref):
    parts, _ = x_runs(cx, cy)

    def cut(s_is_even):
        for part, a_ref, b_ref in ((0, a1_ref, b1_ref), (1, a2_ref, b2_ref)):
            for out_ref, is_east in ((a_ref, s_is_even), (b_ref, not s_is_even)):
                for d, y, count, first in parts[part]:
                    out_ref[pl.ds(first * nf, count * nf), :] = load(cx - d if is_east else d - 1, y, count)

    each_case(lax.rem(lax.axis_index("sim"), 2) == 0, cut)


def cut_shapes(cx, cy, nf, nz):
    sizes = x_runs(cx, cy)[1]
    return [pltpu.VMEM((size * nf, nz), jnp.float32) for size in (sizes[0], sizes[0], sizes[1], sizes[1])]


def columns_kernel(cx, cy, native_ref, out_ref, *cut_refs):
    nf = native_ref.shape[0] // (cx * cy)
    for c in range(cx * cy):
        out_ref[pl.ds(c * nf, nf), :] = native_ref[pl.ds(c, nf, stride=cx * cy), :]
    cut_bricks(cx, cy, nf, lambda x, y, n: out_ref[pl.ds((x * cy + y) * nf, n * nf), :], *cut_refs)


def to_columns(fields):
    nf, cx, cy, nz = fields.shape
    return pl.pallas_call(
        functools.partial(columns_kernel, cx, cy),
        out_shape=[pltpu.VMEM((cx * cy * nf, nz), jnp.float32), *cut_shapes(cx, cy, nf, nz)],
        in_specs=[VMEM],
        out_specs=[VMEM] * 5,
        compiler_params=pltpu.CompilerParams(vmem_limit_bytes=2 * MIB),
        name="to_columns",
    )(*in_vmem(fields.reshape(nf * cx * cy, nz)))


def factors_kernel(dif_ref, sto_ref, after_ref, out_ref):
    del after_ref
    _, nf, nz = out_ref.shape
    field = lax.broadcasted_iota(jnp.int32, (nf, nz), 0)
    for n, ref in enumerate((dif_ref, sto_ref)):
        value = jnp.zeros((nf, nz), jnp.float32)
        for f in range(nf):
            value = jnp.where(field == f, ref[f], value)
        out_ref[n] = value


def field_factors(diffusivity, stoich, nz, after):
    return pl.pallas_call(
        factors_kernel,
        out_shape=pltpu.VMEM((2, diffusivity.shape[0], nz), jnp.float32),
        in_specs=[SMEM, SMEM, pl.BlockSpec(memory_space=pl.ANY)],
        out_specs=VMEM,
        compiler_params=pltpu.CompilerParams(vmem_limit_bytes=MIB),
        name="field_factors",
    )(diffusivity, stoich, after)


def pack_kernel(cx, cy, nf, xa_ref, xb_ref, after_ref, to_a_ref, to_b_ref):
    del after_ref
    runs, size = corner_runs(cx)

    def copy(l_is_even):
        for out_ref, north in ((to_a_ref, l_is_even), (to_b_ref, not l_is_even)):
            for side, brick in enumerate((xa_ref, xb_ref)):
                for d, count, first in runs:
                    row = in_first_part(cx, cy, d, cy - count if north else 0)
                    rows = brick[pl.ds(row * nf, count * nf), :]
                    out_ref[pl.ds((side * size + first) * nf, count * nf), :] = rows

    each_case(lax.rem(lax.axis_index("learn"), 2) == 0, copy)


def pack_corners(xa, xb, after, cx, cy, nf):
    nz = xa.shape[1]
    size = 2 * corner_runs(cx)[1]
    shape = pltpu.VMEM((size * nf, nz), jnp.float32)
    return pl.pallas_call(
        functools.partial(pack_kernel, cx, cy, nf),
        out_shape=(shape, shape),
        in_specs=[VMEM, VMEM, pl.BlockSpec(memory_space=pl.ANY)],
        out_specs=(VMEM, VMEM),
        compiler_params=pltpu.CompilerParams(vmem_limit_bytes=MIB),
        name="pack_corners",
    )(*in_vmem(xa, xb), after)


def load_kernel(source_ref, out_ref, sem):
    copy = pltpu.make_async_copy(source_ref, out_ref, sem)
    copy.start()
    copy.wait()


def load_basis(basis):
    return pl.pallas_call(
        load_kernel,
        out_shape=pltpu.VMEM(basis.shape, basis.dtype),
        in_specs=[pl.BlockSpec(memory_space=pltpu.HBM)],
        out_specs=VMEM,
        scratch_shapes=[pltpu.SemaphoreType.DMA],
        compiler_params=pltpu.CompilerParams(vmem_limit_bytes=MIB),
        name="load_basis",
    )(pltpu.with_memory_space_constraint(basis, pltpu.HBM))


def round_kernel(
    cx, cy, nf, steps, last, own_ref, a1_ref, b1_ref, a2_ref, b2_ref, ya_ref, yb_ref, ca_ref, cb_ref, factors_ref,
    state_ref, snap_ref, *refs,
):
    cut_refs, (u_ref, m_ref, rate_ref) = refs[:-3], refs[-3:]
    nz = own_ref.shape[1]
    reach = 2 * steps
    wide_x, wide_y = cx + 2 * reach, cy + 2 * reach
    s, l = lax.axis_index("sim"), lax.axis_index("learn")
    ns, nl = lax.axis_size("sim"), lax.axis_size("learn")
    even_s, even_l = lax.rem(s, 2) == 0, lax.rem(l, 2) == 0
    has_west, has_east = s > 0, s < ns - 1
    has_south, has_north = l > 0, l < nl - 1

    def place(ref, x0, y0):
        for i in range(cx):
            rows = ref[pl.ds(i * cy * nf, cy * nf), :]
            u_ref[pl.ds(((x0 + i) * wide_y + y0) * nf, cy * nf), :] = rows

    def halo_x(is_east, d):
        return reach + cx + d - 1 if is_east else reach - d

    def clear(x0, x1, y0, y1):
        zeros = jnp.zeros(((y1 - y0) * nf, nz), jnp.float32)

        def trip(x, carry):
            for ref in (u_ref, m_ref):
                ref[pl.ds(pl.multiple_of((x * wide_y + y0) * nf, nf), (y1 - y0) * nf), :] = zeros
            return carry

        lax.fori_loop(x0, x1, trip, 0)

    place(own_ref, reach, reach)
    corners, size = corner_runs(reach)
    parts, _ = x_runs(reach, cy)

    def receive_x(s_is_even):
        for first_ref, rest_ref, is_east in ((a1_ref, a2_ref, s_is_even), (b1_ref, b2_ref, not s_is_even)):

            @pl.when(has_east if is_east else has_west)
            def _(first_ref=first_ref, rest_ref=rest_ref, is_east=is_east):
                for ref, runs in ((first_ref, parts[0]), (rest_ref, parts[1])):
                    for d, y, count, first in runs:
                        rows = ref[pl.ds(first * nf, count * nf), :]
                        u_ref[pl.ds((halo_x(is_east, d) * wide_y + reach + y) * nf, count * nf), :] = rows

    def receive_y(l_is_even):
        for ref, corner, north in ((ya_ref, ca_ref, l_is_even), (yb_ref, cb_ref, not l_is_even)):

            @pl.when(has_north if north else has_south)
            def _(ref=ref, corner=corner, north=north):
                place(ref, reach, reach + cy if north else 0)

                def receive_corners(s_is_even):
                    for side in range(2):
                        for d, count, first in corners:
                            x = halo_x(s_is_even == (side == 0), d)
                            y = reach + cy if north else reach - count
                            rows = corner[pl.ds((side * size + first) * nf, count * nf), :]
                            u_ref[pl.ds((x * wide_y + y) * nf, count * nf), :] = rows

                each_case(even_s, receive_corners)

    each_case(even_s, receive_x)
    each_case(even_l, receive_y)
    pl.when(jnp.logical_not(has_west))(lambda: clear(0, reach, 0, wide_y))
    pl.when(jnp.logical_not(has_east))(lambda: clear(reach + cx, wide_x, 0, wide_y))
    pl.when(jnp.logical_not(has_south))(lambda: clear(0, wide_x, 0, reach))
    pl.when(jnp.logical_not(has_north))(lambda: clear(0, wide_x, reach + cy, wide_y))

    lane = lax.broadcasted_iota(jnp.int32, (nf, nz), 1)
    diffusivity, stoich = factors_ref[0], factors_ref[1]

    def coefficients(dt):
        return (
            1.0 * (dt / time_step) - 6.0 * dt * diffusivity,
            dt * (diffusivity - 0.5 * drift_x),
            dt * (diffusivity + 0.5 * drift_x),
            dt * (diffusivity - 0.5 * drift_y),
            dt * (diffusivity + 0.5 * drift_y),
            jnp.where(lane < nz - 1, dt * (diffusivity - 0.5 * drift_z), 0.0),
            jnp.where(lane > 0, dt * (diffusivity + 0.5 * drift_z), 0.0),
            dt * arrhenius * stoich,
        )

    in_south = jnp.where(has_south, 1.0, 0.0)
    in_north = jnp.where(has_north, 1.0, 0.0)

    def rows_block(src, dst, old, coefs, rows):
        cc, ce, cw, cn, cs, cu, cl, ck = coefs

        def load(x, y):
            return src[pl.ds((x * wide_y + y) * nf, nf), :]

        for k, (x, beyond) in enumerate(rows):
            y_first, width = reach - beyond, cy + 2 * beyond
            for p in range(0, width, nf):
                base = (x * wide_y + y_first + p) * nf
                u0 = src[pl.ds(base, nf, stride=nf), :]
                u1 = src[pl.ds(base + 1, nf, stride=nf), :]
                u7 = src[pl.ds(base + 7, nf, stride=nf), :]
                rate = jnp.tanh(u0) * jnp.tanh(u1) * jnp.exp(-activation / (1.0 + u7 * u7))
                rate_ref[pl.ds(k * (wide_y + nf) + p, nf), :] = rate
        for k, (x, beyond) in enumerate(rows):
            y_first, width = reach - beyond, cy + 2 * beyond
            south, centre = load(x, y_first - 1), load(x, y_first)
            for j in range(width):
                y = y_first + j
                north = load(x, y + 1)
                value = cc * centre + cn * north + cs * south
                value += ce * load(x + 1, y) + cw * load(x - 1, y)
                value += cu * pltpu.roll(centre, nz - 1, 1) + cl * pltpu.roll(centre, 1, 1)
                value += ck * rate_ref[pl.ds(k * (wide_y + nf) + j, nf, stride=0), :]
                if old is not None:
                    value += 0.5 * old[pl.ds((x * wide_y + y) * nf, nf), :]
                if y < reach:
                    value *= in_south
                if y >= reach + cy:
                    value *= in_north
                dst[pl.ds((x * wide_y + y) * nf, nf), :] = value
                south, centre = centre, north

    def stage(src, dst, old, r, coefs):
        group = 4

        def trip(i, carry):
            x0 = reach + i * group
            rows_block(src, dst, old, coefs, [(x0 + k, r) for k in range(group)])
            return carry

        lax.fori_loop(0, cx // group, trip, 0)
        if r:

            @pl.when(has_west)
            def _():
                rows_block(src, dst, old, coefs, [(reach - d, r - d) for d in range(1, r + 1)])

            @pl.when(has_east)
            def _():
                rows_block(src, dst, old, coefs, [(reach + cx - 1 + d, r - d) for d in range(1, r + 1)])

    whole, half = coefficients(time_step), coefficients(0.5 * time_step)
    for t in range(steps):
        r = reach - 1 - 2 * t
        stage(u_ref, m_ref, None, r, whole)
        stage(m_ref, u_ref, u_ref, r - 1, half)
        for x in range(cx):
            for f in range(nf):
                value = u_ref[pl.ds(((reach + x) * wide_y + reach) * nf + f, cy, stride=nf), :]
                snap_ref[f * cx + x, pl.ds(t * cy, cy), :] = value
                if last and t == steps - 1:
                    state_ref[pl.ds((f * cx + x) * cy, cy), :] = value
    if not last:
        for i in range(cx):
            rows = u_ref[pl.ds(((reach + i) * wide_y + reach) * nf, cy * nf), :]
            state_ref[pl.ds(i * cy * nf, cy * nf), :] = rows

        def brick(x, y, count):
            return u_ref[pl.ds(((reach + x) * wide_y + reach + y) * nf, count * nf), :]

        cut_bricks(cx, cy, nf, brick, *cut_refs)


def advance(operands, cx, cy, nf, steps, last):
    nz = operands[0].shape[1]
    wide = (cx + 4 * steps) * (cy + 4 * steps)
    rows = max(cx, 2 * steps) * (cy + 4 * steps + nf)
    shape = (nf * cx * cy, nz)
    cuts = [] if last else cut_shapes(cx, cy, nf, nz)
    return pl.pallas_call(
        functools.partial(round_kernel, cx, cy, nf, steps, last),
        out_shape=[
            pltpu.VMEM(shape, jnp.float32),
            pltpu.VMEM((nf * cx, steps * cy, nz), jnp.float32),
            *cuts,
        ],
        in_specs=[VMEM] * 10,
        out_specs=[VMEM] * (2 + len(cuts)),
        scratch_shapes=[
            pltpu.VMEM((wide * nf, nz), jnp.float32),
            pltpu.VMEM((wide * nf, nz), jnp.float32),
            pltpu.VMEM((rows, nz), jnp.float32),
        ],
        compiler_params=pltpu.CompilerParams(vmem_limit_bytes=8 * MIB),
        name="advance",
    )(*in_vmem(*operands))


def split(value):
    high = value.astype(jnp.bfloat16)
    rest = value - high.astype(jnp.float32)
    middle = rest.astype(jnp.bfloat16)
    return high, middle, (rest - middle.astype(jnp.float32)).astype(jnp.bfloat16)


def project_kernel(cx, cy, steps, copies, basis_ref, snap_ref, *refs):
    earlier_ref, out_ref, acc_ref = refs if copies else (None, *refs)
    modes, nf, _, nz = basis_ref.shape
    pair = 2
    for g in range(nf // pair):
        total = None
        for p in range(cx // 2):
            left, right = [], []
            for f in range(g * pair, (g + 1) * pair):
                left.append(basis_ref[:, f, pl.ds(p * 2 * cy, 2 * cy), :].reshape(modes * 2 * cy, nz))
                rows = snap_ref[pl.ds(f * cx + 2 * p, 2)].reshape(2 * steps * cy, nz)
                right.append(rows.astype(jnp.bfloat16))
            term = lax.dot_general(
                jnp.concatenate(right, axis=1),
                jnp.concatenate(left, axis=1),
                (((1,), (1,)), ((), ())),
                preferred_element_type=jnp.float32,
            )
            total = term if total is None else total + term
        acc_ref[...] = total if g == 0 else acc_ref[...] + total

    lanes = 8 * 2 * cy
    blocks = modes * 2 * cy // lanes
    row = lax.broadcasted_iota(jnp.int32, (cy, lanes), 0)
    column = lax.broadcasted_iota(jnp.int32, (cy, lanes), 1)
    same_y = row == lax.rem(column, cy)
    first_x = lax.rem(column // cy, 2) == 0
    mode_of = lax.broadcasted_iota(jnp.int32, (lanes, modes), 0) // (2 * cy)
    mode = lax.broadcasted_iota(jnp.int32, (lanes, modes), 1)
    summed = None
    for k in range(blocks):
        kept = []
        for t in range(steps):
            west = acc_ref[pl.ds(t * cy, cy), pl.ds(k * lanes, lanes)]
            east = acc_ref[pl.ds((steps + t) * cy, cy), pl.ds(k * lanes, lanes)]
            kept.append(jnp.where(same_y, jnp.where(first_x, west, east), 0.0))
        gather = (mode - 8 * k == mode_of).astype(jnp.bfloat16)
        term = jnp.dot(
            jnp.concatenate(split(jnp.concatenate(kept, axis=0)), axis=0), gather, preferred_element_type=jnp.float32
        )
        summed = term if summed is None else summed + term
    count = steps * cy
    summed = summed[:count] + summed[count : 2 * count] + summed[2 * count :]
    result = jnp.sum(summed.reshape(steps, cy, modes), axis=1)
    if copies:
        both = jnp.concatenate([earlier_ref[...], result], axis=0)
        for n in range(copies):
            out_ref[n] = both
    else:
        out_ref[...] = result


def project(basis, snaps, cx, cy, steps, earlier=None, copies=0):
    modes = basis.shape[0]
    shape = (steps, modes)
    operands = in_vmem(snaps)
    if copies:
        shape = (copies, earlier.shape[0] + steps, modes)
        operands += in_vmem(earlier)
    return pl.pallas_call(
        functools.partial(project_kernel, cx, cy, steps, copies),
        out_shape=jax.ShapeDtypeStruct(shape, jnp.float32) if copies else pltpu.VMEM(shape, jnp.float32),
        in_specs=[VMEM] * (1 + len(operands)),
        out_specs=VMEM,
        scratch_shapes=[pltpu.VMEM((2 * steps * cy, modes * 2 * cy), jnp.float32)],
        compiler_params=pltpu.CompilerParams(vmem_limit_bytes=8 * MIB),
        name="project",
    )(basis, *operands)


def pair_tables(modes):
    upper_pairs = np.triu_indices(modes)
    first_table = np.concatenate([np.zeros(modes), upper_pairs[0] + 1]).astype(np.int32)
    second_table = np.concatenate([np.arange(modes) + 1, upper_pairs[1] + 1]).astype(np.int32)
    return (first_table, second_table)


def infer_kernel(shares_ref, gram_ref, picks_ref, reduced_ref, pod_ref, rhs_ref):
    steps, modes = reduced_ref.shape
    block = rhs_ref.shape[1]
    reduced = shares_ref[0]
    for n in range(1, shares_ref.shape[0]):
        reduced += shares_ref[n]
    reduced_ref[...] = reduced
    transposed = (((0,), (0,)), ((), ()))
    pod_ref[...] = gram_ref[...] + lax.dot_general(
        reduced, reduced, transposed, precision=lax.Precision.HIGHEST, preferred_element_type=jnp.float32
    )
    wide = picks_ref.shape[0]
    padded = jnp.concatenate([reduced, jnp.zeros((steps, wide - modes), jnp.float32)], axis=1)
    lane = lax.broadcasted_iota(jnp.int32, (steps, wide), 1)
    widened = jnp.where(lane == 0, 1.0, pltpu.roll(padded, 1, 1))
    picked = jnp.dot(jnp.concatenate(split(widened), axis=0), picks_ref[...], preferred_element_type=jnp.float32)
    picked = picked[:steps] + picked[steps : 2 * steps] + picked[2 * steps :]
    features = picked[:, :block] * picked[:, picks_ref.shape[1] // 2 :][:, :block]
    row = lax.broadcasted_iota(jnp.int32, (steps, modes), 0)
    changes = jnp.where(row < steps - 1, pltpu.roll(reduced, steps - 1, 0) - reduced, 0.0)
    ch, cm, cl = split(changes)
    fh, fm, fl = split(features)
    rhs_ref[...] = lax.dot_general(
        jnp.concatenate([ch, ch, cm, ch, cm, cl], axis=0),
        jnp.concatenate([fh, fm, fh, fl, fm, fh], axis=0),
        transposed,
        preferred_element_type=jnp.float32,
    )


def picks_kernel(tables_ref, after_ref, out_ref):
    del after_ref
    index = tables_ref[pl.ds(lax.axis_index("learn"), 1), :]
    place = lax.broadcasted_iota(jnp.int32, out_ref.shape, 0)
    out_ref[...] = jnp.where(place == index, 1.0, 0.0).astype(jnp.bfloat16)


def pick_matrices(modes, nl, after):
    tables = np.stack(pair_tables(modes))
    block = tables.shape[1] // nl
    lanes = -(-block // 128) * 128
    tables = tables.reshape(2, nl, block).transpose(1, 0, 2)
    tables = np.pad(tables, ((0, 0), (0, 0), (0, lanes - block)), constant_values=-1).reshape(nl, 2 * lanes)
    wide = -(-(modes + 1) // 128) * 128
    return block, pl.pallas_call(
        picks_kernel,
        out_shape=pltpu.VMEM((wide, 2 * lanes), jnp.bfloat16),
        in_specs=[VMEM, pl.BlockSpec(memory_space=pl.ANY)],
        out_specs=VMEM,
        compiler_params=pltpu.CompilerParams(vmem_limit_bytes=4 * MIB),
        name="pick_matrices",
    )(jnp.asarray(tables), after)


def infer(shares, gram_old, picks, block):
    _, steps, modes = shares.shape
    reduced, pod_gram, rhs = pl.pallas_call(
        infer_kernel,
        out_shape=(
            jax.ShapeDtypeStruct((steps, modes), jnp.float32),
            jax.ShapeDtypeStruct((modes, modes), jnp.float32),
            jax.ShapeDtypeStruct((modes, block), jnp.float32),
        ),
        in_specs=[VMEM] * 3,
        out_specs=(VMEM, VMEM, VMEM),
        compiler_params=pltpu.CompilerParams(vmem_limit_bytes=8 * MIB),
        name="infer",
    )(*in_vmem(shares, gram_old, picks))
    return reduced.T, pod_gram, rhs.T


def swap(value, pairs):
    return lax.ppermute(value, BOTH, pairs)


def mark_kernel(after_ref, out_ref):
    del after_ref
    out_ref[...] = jnp.zeros_like(out_ref)


def mark(after):
    return pl.pallas_call(
        mark_kernel,
        out_shape=pltpu.VMEM((8, after.shape[1]), after.dtype),
        in_specs=[pl.BlockSpec(memory_space=pl.ANY)],
        out_specs=VMEM,
        compiler_params=pltpu.CompilerParams(vmem_limit_bytes=MIB),
        name="mark",
    )(after)


def body(fields, diffusivity, stoich, basis, gram_old):
    nf, cx, cy, nz = fields.shape
    ns, nl = lax.axis_size("sim"), lax.axis_size("learn")
    steps = min(cx, cy) // 2
    rounds = STEPS // steps
    x_even, x_odd, y_even, y_odd, y_far = swaps(ns, nl)
    state, *cuts = to_columns(fields)
    share = None
    for n in range(rounds):
        a1, b1 = swap(cuts[0], x_even), swap(cuts[1], x_odd)
        ya, yb = swap(state, y_even), swap(state, y_odd)
        a2, b2 = swap(cuts[2], x_even), swap(cuts[3], x_odd)
        if n == 0:
            basis = load_basis(basis.reshape(basis.shape[0], nf, cx * cy, nz))
        else:
            part = project(basis, snaps, cx, cy, steps)
            share = part if share is None else jnp.concatenate([share, part], axis=0)
        to_a, to_b = pack_corners(a1, b1, mark(state), cx, cy, nf)
        ca, cb = swap(to_a, y_even), swap(to_b, y_far)
        if n == 0:
            factors = field_factors(diffusivity, stoich, nz, to_b)
        operands = (state, a1, b1, a2, b2, ya, yb, ca, cb, factors)
        state, snaps, *cuts = advance(operands, cx, cy, nf, steps, n == rounds - 1)
    sent = project(basis, snaps, cx, cy, steps, share, ns * nl)
    shares = lax.all_to_all(sent, BOTH, 0, 0)
    block, picks = pick_matrices(gram_old.shape[0], nl, sent)
    reduced, pod_gram, rhs_block = infer(shares, gram_old, picks, block)
    return (state.reshape(fields.shape), reduced, pod_gram, rhs_block)


def solution(mesh):
    in_specs = (P(None, "sim", "learn", None), P(), P(), P(None, None, "sim", "learn", None), P())
    out_specs = (P(None, "sim", "learn", None), P(), P(), P("learn", None))
    return jax.shard_map(body, mesh=mesh, in_specs=in_specs, out_specs=out_specs, check_vma=False)
```
